32 devices in a mesh: region: 4 (over z), member: 8 (over y, x, core).
Axes of the slice: x: 2, y: 2, z: 4, core: 2. Of those that a mesh axis runs over, the one named last changes fastest.
Arguments:
- ensemble: float32 [256, 1024], P('member', 'region'), may hold values from -6 to 6
- obs_value: float32 [2048], replicated, may hold values from -6 to 6
- obs_error: float32 [2048], replicated, may hold values from 0.5 to 2
- obs_region: int32 [2048], replicated, may hold values from 0 to 3
- obs_cell: int32 [2048], replicated, may hold values from 0 to 255
- order: int32 [2048], replicated, may hold values from 0 to 2047, each once
- footprint: int32 [2, 8, 2], P(None, 'region'), may hold values from 0 to 15, as said below
Outputs:
- analysis: float32 [256, 1024], P('member', 'region')
The draws below stay inside these ranges and needn't reach their ends.
Inputs may be any that keep to these rules, and one draw needn't show every extreme that they name: `footprint`: the 2 observation tiles listed for one state tile and batch are different.
All inputs are finite; a program needn't handle non-finite values.
Results may differ from the reference program's by a relative error of at most 0.0003.
Values sent between devices are 32-bit elements; how exact they have to be, the bound alone decides.
A program may use at most 64 MiB of HBM per device.

```python
import math
import jax
import jax.numpy as jnp
from jax import lax

STATE_DEV = 256
NOBS = 1024
BATCHES = 2
STILE = 128
OTILE = 64
FOOT = 2
MEMBERS = 256
CELLS = 1024
NTILES = 8
OBS_TILES = 16
NOBS_ALL = 2048
N_REGION = 4


def draw_footprint(key, part):
    first_key, second_key = jax.random.split(jax.random.fold_in(key, 11))
    first = jax.random.randint(first_key, (BATCHES, NTILES, 1), 0, OBS_TILES, dtype=jnp.int32)
    step_size = jax.random.randint(second_key, (BATCHES, NTILES, 1), 1, OBS_TILES, dtype=jnp.int32)
    second = (first + step_size) % OBS_TILES
    return jnp.concatenate([first, second], axis=2).astype(jnp.int32)


def touch_ends(array, rng, smallest, top_value):
    longest = array.shape.index(max(array.shape))
    spots = []
    for shift in (0, 1):
        where = [jax.random.randint(jax.random.fold_in(rng, axis), (), 0, length) for axis, length in enumerate(array.shape)]
        where[longest] = (where[longest] + shift) % array.shape[longest]
        spots.append(tuple(where))
    return array.at[spots[0]].set(smallest).at[spots[1]].set(top_value)


def level_of(own_key, extent, shards, low, top_value):
    factor_of, own = 1.0, jax.random.fold_in(own_key, 6)
    for dim, shards_of in shards:
        heights = jnp.exp(jax.random.uniform(jax.random.fold_in(own, dim), (shards_of,), jnp.float32, low / len(shards), top_value / len(shards)))
        factor_of = factor_of * jnp.repeat(heights, extent[dim] // shards_of).reshape([-1 if axis == dim else 1 for axis in range(len(extent))])
    return factor_of


def normal_values(own_key, shape, deviation, most, shards=(), kind=jnp.bfloat16):
    entries = deviation * jax.random.normal(own_key, shape, jnp.float32)
    if shards:
        entries = entries * level_of(own_key, shape, shards, -0.22, 0.18)
    return jnp.clip(entries, -most, most).astype(kind)


def setup_inputs(seed: int = 0) -> dict:
    keys = jax.random.split(jax.random.key(seed), 8)
    ensemble = normal_values(keys[0], (MEMBERS, CELLS), 1.0, 6.0, ((0, 8), (1, 4)), jnp.float32)
    obs_value = normal_values(keys[1], (NOBS_ALL,), 1.5, 6.0, (), jnp.float32)
    obs_error = jnp.clip(jnp.exp(jax.random.uniform(keys[2], (NOBS_ALL,), jnp.float32, math.log(0.5), math.log(2.0))), 0.5, 2.0)
    obs_region = touch_ends(jax.random.randint(keys[3], (NOBS_ALL,), 0, N_REGION), jax.random.fold_in(keys[3], 1), 0, N_REGION - 1).astype(jnp.int32)
    obs_cell = touch_ends(jax.random.randint(keys[4], (NOBS_ALL,), 0, STATE_DEV), jax.random.fold_in(keys[4], 1), 0, STATE_DEV - 1).astype(jnp.int32)
    order = jax.random.permutation(keys[5], NOBS_ALL).astype(jnp.int32)
    footprint = draw_footprint(jax.random.fold_in(keys[7], 71), 0)
    return {"ensemble": ensemble, "obs_value": obs_value, "obs_error": obs_error, "obs_region": obs_region, "obs_cell": obs_cell, "order": order, "footprint": footprint}


def reference(ensemble, obs_value, obs_error, obs_region, obs_cell, order, footprint):
    state = ensemble
    offsets = jnp.arange(OTILE, dtype=jnp.int32)
    for batch_no in range(BATCHES):
        chosen = order[batch_no * NOBS:(batch_no + 1) * NOBS]
        grid_cell = (obs_region[chosen] * STATE_DEV + obs_cell[chosen]).astype(jnp.int32)
        priors = jnp.take(state, grid_cell, axis=1)
        obs_mean = lax.optimization_barrier(jnp.sum(priors, axis=0)) / MEMBERS
        obs_pert = priors - obs_mean[None, :]
        obs_var = lax.optimization_barrier(jnp.sum(obs_pert * obs_pert, axis=0)) / (MEMBERS - 1)
        err_var = obs_error[chosen]
        obs_gain = 1.0 / (obs_var + err_var)
        shrink = 1.0 / (1.0 + jnp.sqrt(err_var * obs_gain))
        innovation = obs_value[chosen] - obs_mean
        obs_index = (footprint[batch_no][:, :, None] * OTILE + offsets[None, None, :]).reshape(NTILES, FOOT * OTILE).astype(jnp.int32)
        obs_tiles = jnp.take(obs_pert, obs_index, axis=1)
        state_tiles = state.reshape(MEMBERS, NTILES, STILE)
        covariance = jnp.einsum('mtj,mtc->tjc', obs_tiles, state_tiles, precision=lax.Precision.HIGHEST) / (MEMBERS - 1)
        weight = covariance * obs_gain[obs_index][:, :, None]
        mean_step = jnp.einsum('tjc,tj->tc', weight, innovation[obs_index], precision=lax.Precision.HIGHEST)
        scaled = obs_tiles * shrink[obs_index][None, :, :]
        pert_step = jnp.einsum('mtj,tjc->mtc', scaled, weight, precision=lax.Precision.HIGHEST)
        state = state + mean_step.reshape(CELLS)[None, :] - pert_step.reshape(MEMBERS, CELLS)
    return state
```

```python
import functools

import jax
import jax.numpy as jnp
from jax import lax
from jax.experimental import pallas as pl
from jax.experimental.pallas import tpu as pltpu
from jax.sharding import PartitionSpec as P

NOBS = 1024
BATCHES = 2
STILE = 128
OTILE = 64
FOOT = 2
CORES = 2
LANES = 128
MESH = pl.DeviceIdType.MESH
F32 = jnp.float32
BF16 = jnp.bfloat16
REPLICATED_LIMIT = 4 * 1024 * 1024


def split2(x):
    hi = x.astype(BF16)
    lo = (x - hi.astype(F32)).astype(BF16)
    return hi, lo


def split3(x):
    hi = x.astype(BF16)
    rest = x - hi.astype(F32)
    mid = rest.astype(BF16)
    lo = (rest - mid.astype(F32)).astype(BF16)
    return hi.astype(F32), mid.astype(F32), lo.astype(F32)


def dot(a, b, transposed=False):
    dims = (((1,), (1 if transposed else 0,)), ((), ()))
    return lax.dot_general(a, b, dims, preferred_element_type=F32)


def dot3(a, b, transposed=False):
    a_hi, a_lo = a
    b_hi, b_lo = b
    return dot(a_hi, b_hi, transposed) + (dot(a_hi, b_lo, transposed) + dot(a_lo, b_hi, transposed))


def obs_terms(priors, err, val, members):
    mean = jnp.sum(priors, axis=1, keepdims=True) * (1.0 / members)
    pert = priors - mean
    var = jnp.sum(pert * pert, axis=1, keepdims=True) * (1.0 / (members - 1))
    gain = 1.0 / (var + err)
    shrink = 1.0 / (1.0 + jnp.sqrt(err * gain))
    step = (gain * (1.0 / (members - 1))) * ((val - mean) - shrink * pert)
    return pert, step


def kernel(
    nr, nm, fp_ref, ens_ref, order_ref, region_ref, cell_ref, error_ref, value_ref, out_ref,
    gathered, fp_all, fp_own, feat, hot, state_t, parts, pert_hi, pert_lo, step_hi, step_lo, final,
    send_sem, recv_sem, fp_send, fp_recv,
):
    my_r, my_m = lax.axis_index("region"), lax.axis_index("member")
    md, cd = ens_ref.shape
    members, cells = md * nm, cd * nr
    chips = nm // CORES
    chip, core = my_m // CORES, my_m % CORES
    mate = chip * CORES + (1 - core)
    tiles_dev = cd // STILE
    z_peers = [(my_r + d) % nr for d in range(1, nr)]
    xy_peers = [((chip + e) % chips) * CORES + core for e in range(1, chips)]

    barrier = pltpu.get_barrier_semaphore()
    for r in z_peers:
        pl.semaphore_signal(barrier, inc=1, device_id=(r, my_m), device_id_type=MESH)
    for m in xy_peers + [mate]:
        pl.semaphore_signal(barrier, inc=1, device_id=(my_r, m), device_id_type=MESH)
    slots = BATCHES * tiles_dev * FOOT
    lane8 = lax.broadcasted_iota(jnp.int32, (8, LANES), 1)
    fp_sent, fp_here = [jnp.zeros((8, LANES), jnp.int32)] * 2
    slot = 0
    for b in range(BATCHES):
        for t in range(tiles_dev):
            for f in range(FOOT):
                tile = fp_ref[b, t, f]
                fp_sent = jnp.where(lane8 == my_r * slots + slot, tile, fp_sent)
                fp_here = jnp.where(lane8 == nr * slots + slot, tile, fp_here)
                slot += 1
    fp_own[...] = fp_sent
    pl.semaphore_wait(barrier, len(z_peers) + len(xy_peers) + 1)

    sent = []

    def block(r, m):
        return gathered.at[r, pl.ds(pl.multiple_of(m * md, md), md), :]

    def send(r, m, to, own=False):
        copy = pltpu.make_async_remote_copy(
            src_ref=ens_ref if own else block(r, m),
            dst_ref=block(r, m),
            send_sem=send_sem.at[len(sent)],
            recv_sem=recv_sem.at[r, m],
            device_id=to,
            device_id_type=MESH,
        )
        copy.start()
        sent.append(copy)

    def arrived(r, m):
        pltpu.make_async_remote_copy(
            src_ref=block(r, m),
            dst_ref=block(r, m),
            send_sem=send_sem.at[0],
            recv_sem=recv_sem.at[r, m],
            device_id=(my_r, mate),
            device_id_type=MESH,
        ).wait_recv()

    def fp_copy(i, r_from, r_to):
        return pltpu.make_async_remote_copy(
            src_ref=fp_own,
            dst_ref=fp_all.at[r_from],
            send_sem=fp_send.at[i],
            recv_sem=fp_recv.at[r_from],
            device_id=(r_to, my_m),
            device_id_type=MESH,
        )

    for r in z_peers:
        send(my_r, my_m, (r, my_m), own=True)
    for m in xy_peers:
        send(my_r, my_m, (my_r, m), own=True)
    send(my_r, my_m, (my_r, mate), own=True)
    for i, r in enumerate(z_peers):
        fp_copy(i, my_r, r).start()
    gathered[my_r, pl.ds(pl.multiple_of(my_m * md, md), md), :] = ens_ref[...]

    rows = order_ref.shape[0]
    table = jnp.concatenate(
        [region_ref[...].astype(F32), cell_ref[...].astype(F32)]
        + list(split3(error_ref[...]))
        + list(split3(value_ref[...])),
        axis=0,
    )
    table_t = jnp.transpose(table).astype(BF16)
    width = table.shape[0]
    order_t = jnp.transpose(
        jnp.concatenate([order_ref[...].astype(F32), jnp.zeros((LANES - rows, LANES), F32)], axis=0)
    ).astype(jnp.int32)
    lane = lax.broadcasted_iota(jnp.int32, (LANES, LANES), 1)
    line = lax.broadcasted_iota(jnp.int32, (LANES, LANES), 0)
    wide_lane = lax.broadcasted_iota(jnp.int32, (LANES, width), 1)
    kind = lax.broadcasted_iota(jnp.int32, (width, LANES), 0) // rows
    column = lax.broadcasted_iota(jnp.int32, (width, LANES), 1)
    collect = jnp.where((kind == 0) & (column == 0), float(cd), 0.0)
    collect = jnp.where((kind == 1) & (column == 0), 1.0, collect)
    collect = jnp.where((kind >= 2) & (kind <= 4) & (column == 1), 1.0, collect)
    collect = jnp.where((kind >= 5) & (column == 2), 1.0, collect).astype(BF16)
    for i, r in enumerate(z_peers):
        fp_copy(i, r, r).wait_recv()
        fp_here = fp_here + fp_all[r]
    tile_of = (fp_here + fp_sent)[0:1, :]
    lane1 = lax.broadcasted_iota(jnp.int32, (1, LANES), 1)
    batch_of = lane1 % slots // (tiles_dev * FOOT)
    half = LANES // OTILE
    pick = jnp.where(line == batch_of * (NOBS // LANES) + tile_of // half, 1.0, 0.0).astype(BF16)
    high_all = dot((order_t // LANES).astype(F32).astype(BF16), pick)
    low_all = dot((order_t % LANES).astype(F32).astype(BF16), pick)
    upper = tile_of % half == 1
    high_all = jnp.where(upper, high_all[OTILE:, :], high_all[:OTILE, :]).astype(jnp.int32)
    low_all = jnp.where(upper, low_all[OTILE:, :], low_all[:OTILE, :]).astype(jnp.int32)
    wide = lax.broadcasted_iota(jnp.int32, (LANES, cells), 1)
    firsts = [r * slots + t * FOOT for r in range(nr) for t in range(tiles_dev)]
    firsts += [nr * slots + (tiles_dev + t) * FOOT for t in range(tiles_dev)]
    for q, first in enumerate(firsts):
        here = slice(q * LANES, (q + 1) * LANES)
        high, low = [
            jnp.concatenate([v[:, first + f : first + f + 1] for f in range(FOOT)], axis=0)
            for v in (high_all, low_all)
        ]
        found = dot(jnp.where(lane == low, 1.0, 0.0).astype(BF16), table_t)
        found = jnp.where(wide_lane % rows == high, found, 0.0).astype(BF16)
        found = dot(found, collect)
        feat[here, :] = found
        hot[here, :] = jnp.where(wide == found[:, 0:1].astype(jnp.int32), 1.0, 0.0).astype(BF16)

    for r in z_peers:
        arrived(r, my_m)
        for m in xy_peers:
            send(r, my_m, (my_r, m))
        send(r, my_m, (my_r, mate))
    for r in [my_r] + z_peers:
        for m in xy_peers:
            arrived(r, m)
            send(r, m, (my_r, mate))
    mate_blocks = [mate] + [((chip + e) % chips) * CORES + (1 - core) for e in range(1, chips)]
    for r in [my_r] + z_peers:
        for m in mate_blocks:
            arrived(r, m)

    for r in range(nr):
        turned = jnp.transpose(gathered[r])
        state_t[r * cd : (r + 1) * cd, :] = turned
        hi, lo = split2(turned)
        parts[r * cd : (r + 1) * cd, :members] = hi
        parts[r * cd : (r + 1) * cd, members:] = lo

    firsts = nr * tiles_dev * STILE
    both = dot(hot[:firsts, :], parts[...])
    pert, step = obs_terms(
        both[:, :members] + both[:, members:], feat[:firsts, 1:2], feat[:firsts, 2:3], members
    )
    pert_hi[...], pert_lo[...] = split2(pert)
    step_hi[...], step_lo[...] = split2(step)

    for r in range(nr):
        for t in range(tiles_dev):
            first = r * cd + t * STILE
            obs = slice((r * tiles_dev + t) * STILE, (r * tiles_dev + t + 1) * STILE)
            p_hi, p_lo, s_hi, s_lo = [ref[obs, :] for ref in (pert_hi, pert_lo, step_hi, step_lo)]
            own = (parts[first : first + STILE, :members], parts[first : first + STILE, members:])
            cov = dot3(own, (p_hi, p_lo), transposed=True)
            new = state_t[first : first + STILE, :] + dot3(split2(cov), (s_hi, s_lo))
            state_t[first : first + STILE, :] = new
            hi, lo = split2(new)
            parts[first : first + STILE, :members] = hi
            parts[first : first + STILE, members:] = lo

    for t in range(tiles_dev):
        obs = slice(firsts + t * STILE, firsts + (t + 1) * STILE)
        both = dot(hot[obs, :], parts[...])
        pert, step = obs_terms(
            both[:, :members] + both[:, members:], feat[obs, 1:2], feat[obs, 2:3], members
        )
        here = pl.ds(pl.multiple_of(my_r * cd + t * STILE, STILE), STILE)
        cov = dot3((parts[here, :members], parts[here, members:]), split2(pert), transposed=True)
        new = state_t[here, :] + dot3(split2(cov), split2(step))
        final[:, t * STILE : (t + 1) * STILE] = jnp.transpose(new)
    out_ref[...] = final[pl.ds(pl.multiple_of(my_m * md, md), md), :]

    for copy in sent:
        copy.wait_send()
    for i, r in enumerate(z_peers):
        fp_copy(i, my_r, r).wait_send()


def replicated(nr, nm, ensemble, obs_value, obs_error, obs_region, obs_cell, order, footprint):
    md, cd = ensemble.shape
    members, cells = md * nm, cd * nr
    total = order.shape[0]
    lines = [v.reshape(total // LANES, LANES) for v in (order, obs_region, obs_cell, obs_error, obs_value)]
    vmem = pl.BlockSpec(memory_space=pltpu.VMEM)
    chips = nm // CORES
    sends = (nr - 1) + nr * (chips - 1) + nr * chips
    return pl.pallas_call(
        functools.partial(kernel, nr, nm),
        out_shape=jax.ShapeDtypeStruct((md, cd), F32),
        in_specs=[pl.BlockSpec(memory_space=pltpu.SMEM)] + [vmem] * 6,
        out_specs=vmem,
        scratch_shapes=[
            pltpu.VMEM((nr, members, cd), F32),
            pltpu.VMEM((nr, 8, LANES), jnp.int32),
            pltpu.VMEM((8, LANES), jnp.int32),
            pltpu.VMEM((cells + cd, LANES), F32),
            pltpu.VMEM((cells + cd, cells), BF16),
            pltpu.VMEM((cells, members), F32),
            pltpu.VMEM((cells, 2 * members), BF16),
            pltpu.VMEM((cells, members), BF16),
            pltpu.VMEM((cells, members), BF16),
            pltpu.VMEM((cells, members), BF16),
            pltpu.VMEM((cells, members), BF16),
            pltpu.VMEM((members, cd), F32),
            pltpu.SemaphoreType.DMA((sends,)),
            pltpu.SemaphoreType.DMA((nr, nm)),
            pltpu.SemaphoreType.DMA((nr,)),
            pltpu.SemaphoreType.DMA((nr,)),
        ],
        compiler_params=pltpu.CompilerParams(
            collective_id=0, has_side_effects=True, vmem_limit_bytes=48 * 1024 * 1024
        ),
    )(footprint, ensemble, *lines)


def sharded(ensemble, obs_value, obs_error, obs_region, obs_cell, order, footprint):
    mem_dev, cell_count = ensemble.shape
    members = mem_dev * lax.axis_size("member")
    tile_count = cell_count // STILE
    state = ensemble
    region = lax.axis_index("region")
    offsets = jnp.arange(OTILE, dtype=jnp.int32)
    for batch_no in range(BATCHES):
        chosen = order[batch_no * NOBS : (batch_no + 1) * NOBS]
        owned_here = obs_region[chosen] == region
        picked = jnp.where(owned_here[None, :], jnp.take(state, obs_cell[chosen], axis=1), 0.0)
        priors = lax.psum(picked, "region")
        obs_index = (footprint[batch_no][:, :, None] * OTILE + offsets[None, None, :]).reshape(
            tile_count, FOOT * OTILE
        )
        state_tiles = state.reshape(mem_dev, tile_count, STILE)
        s_one = jnp.sum(priors, axis=0)
        s_two = jnp.sum(priors * priors, axis=0)
        s_one, s_two = lax.psum((s_one, s_two), "member")
        obs_mean = s_one / members
        obs_pert = priors - obs_mean[None, :]
        obs_tiles = jnp.take(obs_pert, obs_index, axis=1)
        partial_value = jnp.einsum(
            "mtj,mtc->tjc", obs_tiles, state_tiles, precision=lax.Precision.HIGHEST
        )
        summed = lax.psum(partial_value, "member")
        covariance = summed / (members - 1)
        obs_var = (s_two - s_one * obs_mean) / (members - 1)
        err_var = obs_error[chosen]
        obs_gain = 1.0 / (obs_var + err_var)
        shrink = 1.0 / (1.0 + jnp.sqrt(err_var * obs_gain))
        innovation = obs_value[chosen] - obs_mean
        weight = covariance * obs_gain[obs_index][:, :, None]
        mean_step = jnp.einsum(
            "tjc,tj->tc", weight, innovation[obs_index], precision=lax.Precision.HIGHEST
        )
        scaled = obs_tiles * shrink[obs_index][None, :, :]
        pert_step = jnp.einsum("mtj,tjc->mtc", scaled, weight, precision=lax.Precision.HIGHEST)
        state = (
            state + mean_step.reshape(cell_count)[None, :] - pert_step.reshape(mem_dev, cell_count)
        )
    return state


def solution(mesh):
    nr, nm = mesh.shape["region"], mesh.shape["member"]

    def per_device(ensemble, *rest):
        if 4 * ensemble.size * nr * nm <= REPLICATED_LIMIT:
            return replicated(nr, nm, ensemble, *rest)
        return sharded(ensemble, *rest)

    in_specs = (P("member", "region"), P(), P(), P(), P(), P(), P(None, "region", None))
    out_specs = P("member", "region")
    return jax.shard_map(
        per_device, mesh=mesh, in_specs=in_specs, out_specs=out_specs, check_vma=False
    )
```

```python
import functools

import jax
import jax.numpy as jnp
from jax import lax
from jax.experimental import pallas as pl
from jax.experimental.pallas import tpu as pltpu
from jax.sharding import PartitionSpec as P

NOBS = 1024
BATCHES = 2
STILE = 128
OTILE = 64
FOOT = 2
CORES = 2
LANES = 128
MESH = pl.DeviceIdType.MESH
F32 = jnp.float32
BF16 = jnp.bfloat16
REPLICATED_LIMIT = 4 * 1024 * 1024


def split2(x):
    hi = x.astype(BF16)
    lo = (x - hi.astype(F32)).astype(BF16)
    return hi, lo


def split3(x):
    hi = x.astype(BF16)
    rest = x - hi.astype(F32)
    mid = rest.astype(BF16)
    lo = (rest - mid.astype(F32)).astype(BF16)
    return hi.astype(F32), mid.astype(F32), lo.astype(F32)


def dot(a, b, transposed=False):
    dims = (((1,), (1 if transposed else 0,)), ((), ()))
    return lax.dot_general(a, b, dims, preferred_element_type=F32)


def dot3(a, b, transposed=False):
    a_hi, a_lo = a
    b_hi, b_lo = b
    return dot(a_hi, b_hi, transposed) + (dot(a_hi, b_lo, transposed) + dot(a_lo, b_hi, transposed))


def obs_terms(priors, err, val, members):
    mean = jnp.sum(priors, axis=1, keepdims=True) * (1.0 / members)
    pert = priors - mean
    var = jnp.sum(pert * pert, axis=1, keepdims=True) * (1.0 / (members - 1))
    gain = 1.0 / (var + err)
    shrink = 1.0 / (1.0 + jnp.sqrt(err * gain))
    step = (gain * (1.0 / (members - 1))) * ((val - mean) - shrink * pert)
    return pert, step


def kernel(
    nr, nm, fp_hbm, ens_hbm, order_hbm, region_hbm, cell_hbm, error_hbm, value_hbm, out_ref,
    fp_ref, order_ref, region_ref, cell_ref, error_ref, value_ref, load_sem, gathered, fp_all, fp_own, feat, hot, state_t, parts, pert_hi, pert_lo, step_hi, step_lo, final,
    send_sem, recv_sem, fp_send, fp_recv,
):
    my_r, my_m = lax.axis_index("region"), lax.axis_index("member")
    md, cd = ens_hbm.shape
    members, cells = md * nm, cd * nr
    chips = nm // CORES
    chip, core = my_m // CORES, my_m % CORES
    mate = chip * CORES + (1 - core)
    tiles_dev = cd // STILE
    z_peers = [(my_r + d) % nr for d in range(1, nr)]
    xy_peers = [((chip + e) % chips) * CORES + core for e in range(1, chips)]

    own_block = gathered.at[my_r, pl.ds(pl.multiple_of(my_m * md, md), md), :]
    loads = [
        pltpu.make_async_copy(src, dst, load_sem.at[i])
        for i, (src, dst) in enumerate(
            [
                (fp_hbm, fp_ref),
                (ens_hbm, own_block),
                (order_hbm, order_ref),
                (region_hbm, region_ref),
                (cell_hbm, cell_ref),
                (error_hbm, error_ref),
                (value_hbm, value_ref),
            ]
        )
    ]
    for load in loads:
        load.start()
    barrier = pltpu.get_barrier_semaphore()
    for r in z_peers:
        pl.semaphore_signal(barrier, inc=1, device_id=(r, my_m), device_id_type=MESH)
    for m in xy_peers + [mate]:
        pl.semaphore_signal(barrier, inc=1, device_id=(my_r, m), device_id_type=MESH)
    loads[0].wait()
    slots = BATCHES * tiles_dev * FOOT
    lane8 = lax.broadcasted_iota(jnp.int32, (8, LANES), 1)
    fp_sent, fp_here = [jnp.zeros((8, LANES), jnp.int32)] * 2
    slot = 0
    for b in range(BATCHES):
        for t in range(tiles_dev):
            for f in range(FOOT):
                tile = fp_ref[b, t, f]
                fp_sent = jnp.where(lane8 == my_r * slots + slot, tile, fp_sent)
                fp_here = jnp.where(lane8 == nr * slots + slot, tile, fp_here)
                slot += 1
    fp_own[...] = fp_sent
    loads[1].wait()
    pl.semaphore_wait(barrier, len(z_peers) + len(xy_peers) + 1)

    sent = []

    def block(r, m):
        return gathered.at[r, pl.ds(pl.multiple_of(m * md, md), md), :]

    def send(r, m, to):
        copy = pltpu.make_async_remote_copy(
            src_ref=block(r, m),
            dst_ref=block(r, m),
            send_sem=send_sem.at[len(sent)],
            recv_sem=recv_sem.at[r, m],
            device_id=to,
            device_id_type=MESH,
        )
        copy.start()
        sent.append(copy)

    def arrived(r, m):
        pltpu.make_async_remote_copy(
            src_ref=block(r, m),
            dst_ref=block(r, m),
            send_sem=send_sem.at[0],
            recv_sem=recv_sem.at[r, m],
            device_id=(my_r, mate),
            device_id_type=MESH,
        ).wait_recv()

    def fp_copy(i, r_from, r_to):
        return pltpu.make_async_remote_copy(
            src_ref=fp_own,
            dst_ref=fp_all.at[r_from],
            send_sem=fp_send.at[i],
            recv_sem=fp_recv.at[r_from],
            device_id=(r_to, my_m),
            device_id_type=MESH,
        )

    for r in z_peers:
        send(my_r, my_m, (r, my_m))
    for m in xy_peers:
        send(my_r, my_m, (my_r, m))
    send(my_r, my_m, (my_r, mate))
    for i, r in enumerate(z_peers):
        fp_copy(i, my_r, r).start()
    for load in loads[2:]:
        load.wait()

    rows = order_ref.shape[0]
    table = jnp.concatenate(
        [region_ref[...].astype(F32), cell_ref[...].astype(F32)]
        + list(split3(error_ref[...]))
        + list(split3(value_ref[...])),
        axis=0,
    )
    table_t = jnp.transpose(table).astype(BF16)
    width = table.shape[0]
    order_t = jnp.transpose(
        jnp.concatenate([order_ref[...].astype(F32), jnp.zeros((LANES - rows, LANES), F32)], axis=0)
    ).astype(jnp.int32)
    lane = lax.broadcasted_iota(jnp.int32, (LANES, LANES), 1)
    line = lax.broadcasted_iota(jnp.int32, (LANES, LANES), 0)
    wide_lane = lax.broadcasted_iota(jnp.int32, (LANES, width), 1)
    kind = lax.broadcasted_iota(jnp.int32, (width, LANES), 0) // rows
    column = lax.broadcasted_iota(jnp.int32, (width, LANES), 1)
    collect = jnp.where((kind == 0) & (column == 0), float(cd), 0.0)
    collect = jnp.where((kind == 1) & (column == 0), 1.0, collect)
    collect = jnp.where((kind >= 2) & (kind <= 4) & (column == 1), 1.0, collect)
    collect = jnp.where((kind >= 5) & (column == 2), 1.0, collect).astype(BF16)
    for i, r in enumerate(z_peers):
        fp_copy(i, r, r).wait_recv()
        fp_here = fp_here + fp_all[r]
    tile_of = (fp_here + fp_sent)[0:1, :]
    lane1 = lax.broadcasted_iota(jnp.int32, (1, LANES), 1)
    batch_of = lane1 % slots // (tiles_dev * FOOT)
    half = LANES // OTILE
    pick = jnp.where(line == batch_of * (NOBS // LANES) + tile_of // half, 1.0, 0.0).astype(BF16)
    high_all = dot((order_t // LANES).astype(F32).astype(BF16), pick)
    low_all = dot((order_t % LANES).astype(F32).astype(BF16), pick)
    upper = tile_of % half == 1
    high_all = jnp.where(upper, high_all[OTILE:, :], high_all[:OTILE, :]).astype(jnp.int32)
    low_all = jnp.where(upper, low_all[OTILE:, :], low_all[:OTILE, :]).astype(jnp.int32)
    wide = lax.broadcasted_iota(jnp.int32, (LANES, cells), 1)
    firsts = [r * slots + t * FOOT for r in range(nr) for t in range(tiles_dev)]
    firsts += [nr * slots + (tiles_dev + t) * FOOT for t in range(tiles_dev)]
    for q, first in enumerate(firsts):
        here = slice(q * LANES, (q + 1) * LANES)
        high, low = [
            jnp.concatenate([v[:, first + f : first + f + 1] for f in range(FOOT)], axis=0)
            for v in (high_all, low_all)
        ]
        found = dot(jnp.where(lane == low, 1.0, 0.0).astype(BF16), table_t)
        found = jnp.where(wide_lane % rows == high, found, 0.0).astype(BF16)
        found = dot(found, collect)
        feat[here, :] = found
        hot[here, :] = jnp.where(wide == found[:, 0:1].astype(jnp.int32), 1.0, 0.0).astype(BF16)

    for r in z_peers:
        arrived(r, my_m)
        for m in xy_peers:
            send(r, my_m, (my_r, m))
        send(r, my_m, (my_r, mate))
    for r in [my_r] + z_peers:
        for m in xy_peers:
            arrived(r, m)
            send(r, m, (my_r, mate))
    mate_blocks = [mate] + [((chip + e) % chips) * CORES + (1 - core) for e in range(1, chips)]
    for r in [my_r] + z_peers:
        for m in mate_blocks:
            arrived(r, m)

    for r in range(nr):
        turned = jnp.transpose(gathered[r])
        state_t[r * cd : (r + 1) * cd, :] = turned
        hi, lo = split2(turned)
        parts[r * cd : (r + 1) * cd, :members] = hi
        parts[r * cd : (r + 1) * cd, members:] = lo

    firsts = nr * tiles_dev * STILE
    both = dot(hot[:firsts, :], parts[...])
    pert, step = obs_terms(
        both[:, :members] + both[:, members:], feat[:firsts, 1:2], feat[:firsts, 2:3], members
    )
    pert_hi[...], pert_lo[...] = split2(pert)
    step_hi[...], step_lo[...] = split2(step)

    for r in range(nr):
        for t in range(tiles_dev):
            first = r * cd + t * STILE
            obs = slice((r * tiles_dev + t) * STILE, (r * tiles_dev + t + 1) * STILE)
            p_hi, p_lo, s_hi, s_lo = [ref[obs, :] for ref in (pert_hi, pert_lo, step_hi, step_lo)]
            own = (parts[first : first + STILE, :members], parts[first : first + STILE, members:])
            cov = dot3(own, (p_hi, p_lo), transposed=True)
            new = state_t[first : first + STILE, :] + dot3(split2(cov), (s_hi, s_lo))
            state_t[first : first + STILE, :] = new
            hi, lo = split2(new)
            parts[first : first + STILE, :members] = hi
            parts[first : first + STILE, members:] = lo

    for t in range(tiles_dev):
        obs = slice(firsts + t * STILE, firsts + (t + 1) * STILE)
        both = dot(hot[obs, :], parts[...])
        pert, step = obs_terms(
            both[:, :members] + both[:, members:], feat[obs, 1:2], feat[obs, 2:3], members
        )
        here = pl.ds(pl.multiple_of(my_r * cd + t * STILE, STILE), STILE)
        cov = dot3((parts[here, :members], parts[here, members:]), split2(pert), transposed=True)
        new = state_t[here, :] + dot3(split2(cov), split2(step))
        final[:, t * STILE : (t + 1) * STILE] = jnp.transpose(new)
    out_ref[...] = final[pl.ds(pl.multiple_of(my_m * md, md), md), :]

    for copy in sent:
        copy.wait_send()
    for i, r in enumerate(z_peers):
        fp_copy(i, my_r, r).wait_send()


def replicated(nr, nm, ensemble, obs_value, obs_error, obs_region, obs_cell, order, footprint):
    md, cd = ensemble.shape
    members, cells = md * nm, cd * nr
    total = order.shape[0]
    lines = [v.reshape(total // LANES, LANES) for v in (order, obs_region, obs_cell, obs_error, obs_value)]
    line = (total // LANES, LANES)
    chips = nm // CORES
    sends = (nr - 1) + nr * (chips - 1) + nr * chips
    return pl.pallas_call(
        functools.partial(kernel, nr, nm),
        out_shape=jax.ShapeDtypeStruct((md, cd), F32),
        in_specs=[pl.BlockSpec(memory_space=pltpu.HBM)] * 7,
        out_specs=pl.BlockSpec(memory_space=pltpu.VMEM),
        scratch_shapes=[
            pltpu.SMEM(footprint.shape, jnp.int32),
            pltpu.VMEM(line, jnp.int32),
            pltpu.VMEM(line, jnp.int32),
            pltpu.VMEM(line, jnp.int32),
            pltpu.VMEM(line, F32),
            pltpu.VMEM(line, F32),
            pltpu.SemaphoreType.DMA((7,)),
            pltpu.VMEM((nr, members, cd), F32),
            pltpu.VMEM((nr, 8, LANES), jnp.int32),
            pltpu.VMEM((8, LANES), jnp.int32),
            pltpu.VMEM((cells + cd, LANES), F32),
            pltpu.VMEM((cells + cd, cells), BF16),
            pltpu.VMEM((cells, members), F32),
            pltpu.VMEM((cells, 2 * members), BF16),
            pltpu.VMEM((cells, members), BF16),
            pltpu.VMEM((cells, members), BF16),
            pltpu.VMEM((cells, members), BF16),
            pltpu.VMEM((cells, members), BF16),
            pltpu.VMEM((members, cd), F32),
            pltpu.SemaphoreType.DMA((sends,)),
            pltpu.SemaphoreType.DMA((nr, nm)),
            pltpu.SemaphoreType.DMA((nr,)),
            pltpu.SemaphoreType.DMA((nr,)),
        ],
        compiler_params=pltpu.CompilerParams(
            collective_id=0, has_side_effects=True, vmem_limit_bytes=64 * 1024 * 1024
        ),
    )(footprint, ensemble, *lines)


def sharded(ensemble, obs_value, obs_error, obs_region, obs_cell, order, footprint):
    mem_dev, cell_count = ensemble.shape
    members = mem_dev * lax.axis_size("member")
    tile_count = cell_count // STILE
    state = ensemble
    region = lax.axis_index("region")
    offsets = jnp.arange(OTILE, dtype=jnp.int32)
    for batch_no in range(BATCHES):
        chosen = order[batch_no * NOBS : (batch_no + 1) * NOBS]
        owned_here = obs_region[chosen] == region
        picked = jnp.where(owned_here[None, :], jnp.take(state, obs_cell[chosen], axis=1), 0.0)
        priors = lax.psum(picked, "region")
        obs_index = (footprint[batch_no][:, :, None] * OTILE + offsets[None, None, :]).reshape(
            tile_count, FOOT * OTILE
        )
        state_tiles = state.reshape(mem_dev, tile_count, STILE)
        s_one = jnp.sum(priors, axis=0)
        s_two = jnp.sum(priors * priors, axis=0)
        s_one, s_two = lax.psum((s_one, s_two), "member")
        obs_mean = s_one / members
        obs_pert = priors - obs_mean[None, :]
        obs_tiles = jnp.take(obs_pert, obs_index, axis=1)
        partial_value = jnp.einsum(
            "mtj,mtc->tjc", obs_tiles, state_tiles, precision=lax.Precision.HIGHEST
        )
        summed = lax.psum(partial_value, "member")
        covariance = summed / (members - 1)
        obs_var = (s_two - s_one * obs_mean) / (members - 1)
        err_var = obs_error[chosen]
        obs_gain = 1.0 / (obs_var + err_var)
        shrink = 1.0 / (1.0 + jnp.sqrt(err_var * obs_gain))
        innovation = obs_value[chosen] - obs_mean
        weight = covariance * obs_gain[obs_index][:, :, None]
        mean_step = jnp.einsum(
            "tjc,tj->tc", weight, innovation[obs_index], precision=lax.Precision.HIGHEST
        )
        scaled = obs_tiles * shrink[obs_index][None, :, :]
        pert_step = jnp.einsum("mtj,tjc->mtc", scaled, weight, precision=lax.Precision.HIGHEST)
        state = (
            state + mean_step.reshape(cell_count)[None, :] - pert_step.reshape(mem_dev, cell_count)
        )
    return state


def solution(mesh):
    nr, nm = mesh.shape["region"], mesh.shape["member"]

    def per_device(ensemble, *rest):
        if 4 * ensemble.size * nr * nm <= REPLICATED_LIMIT:
            return replicated(nr, nm, ensemble, *rest)
        return sharded(ensemble, *rest)

    in_specs = (P("member", "region"), P(), P(), P(), P(), P(), P(None, "region", None))
    out_specs = P("member", "region")
    return jax.shard_map(
        per_device, mesh=mesh, in_specs=in_specs, out_specs=out_specs, check_vma=False
    )
```

```python
import functools

import jax
import jax.numpy as jnp
from jax import lax
from jax.experimental import pallas as pl
from jax.experimental.pallas import tpu as pltpu
from jax.sharding import PartitionSpec as P

NOBS = 1024
BATCHES = 2
STILE = 128
OTILE = 64
FOOT = 2
CORES = 2
LANES = 128
MESH = pl.DeviceIdType.MESH
F32 = jnp.float32
BF16 = jnp.bfloat16
REPLICATED_LIMIT = 4 * 1024 * 1024


def split2(x):
    hi = x.astype(BF16)
    lo = (x - hi.astype(F32)).astype(BF16)
    return hi, lo


def split3(x):
    hi = x.astype(BF16)
    rest = x - hi.astype(F32)
    mid = rest.astype(BF16)
    lo = (rest - mid.astype(F32)).astype(BF16)
    return hi.astype(F32), mid.astype(F32), lo.astype(F32)


def dot(a, b, transposed=False):
    dims = (((1,), (1 if transposed else 0,)), ((), ()))
    return lax.dot_general(a, b, dims, preferred_element_type=F32)


def dot3(a, b, transposed=False):
    a_hi, a_lo = a
    b_hi, b_lo = b
    return dot(a_hi, b_hi, transposed) + (dot(a_hi, b_lo, transposed) + dot(a_lo, b_hi, transposed))


def obs_terms(priors, err, val, members):
    mean = jnp.sum(priors, axis=1, keepdims=True) * (1.0 / members)
    pert = priors - mean
    var = jnp.sum(pert * pert, axis=1, keepdims=True) * (1.0 / (members - 1))
    gain = 1.0 / (var + err)
    shrink = 1.0 / (1.0 + jnp.sqrt(err * gain))
    step = (gain * (1.0 / (members - 1))) * ((val - mean) - shrink * pert)
    return pert, step


def kernel(
    nr, nm, fp_hbm, ens_hbm, order_hbm, region_hbm, cell_hbm, error_hbm, value_hbm, out_ref,
    fp_ref, order_ref, region_ref, cell_ref, error_ref, value_ref, load_sem, gathered, fp_all, fp_own, feat, hot, priors, state_t, parts, pert_hi, pert_lo, step_hi, step_lo, final,
    send_sem, recv_sem, fp_send, fp_recv,
):
    my_r, my_m = lax.axis_index("region"), lax.axis_index("member")
    md, cd = ens_hbm.shape
    members, cells = md * nm, cd * nr
    chips = nm // CORES
    chip, core = my_m // CORES, my_m % CORES
    mate = chip * CORES + (1 - core)
    tiles_dev = cd // STILE
    z_peers = [(my_r + d) % nr for d in sorted(range(1, nr), key=lambda d: min(d, nr - d))]
    xy_peers = [((chip + e) % chips) * CORES + core for e in range(1, chips)]

    own_block = gathered.at[my_r, pl.ds(pl.multiple_of(my_m * md, md), md), :]
    loads = [
        pltpu.make_async_copy(src, dst, load_sem.at[i])
        for i, (src, dst) in enumerate(
            [
                (fp_hbm, fp_ref),
                (ens_hbm, own_block),
                (order_hbm, order_ref),
                (region_hbm, region_ref),
                (cell_hbm, cell_ref),
                (error_hbm, error_ref),
                (value_hbm, value_ref),
            ]
        )
    ]
    for load in loads:
        load.start()
    barrier = pltpu.get_barrier_semaphore()
    for r in z_peers:
        pl.semaphore_signal(barrier, inc=1, device_id=(r, my_m), device_id_type=MESH)
    for m in xy_peers + [mate]:
        pl.semaphore_signal(barrier, inc=1, device_id=(my_r, m), device_id_type=MESH)
    loads[0].wait()
    slots = BATCHES * tiles_dev * FOOT
    lane8 = lax.broadcasted_iota(jnp.int32, (8, LANES), 1)
    fp_sent, fp_here = [jnp.zeros((8, LANES), jnp.int32)] * 2
    slot = 0
    for b in range(BATCHES):
        for t in range(tiles_dev):
            for f in range(FOOT):
                tile = fp_ref[b, t, f]
                fp_sent = jnp.where(lane8 == my_r * slots + slot, tile, fp_sent)
                fp_here = jnp.where(lane8 == nr * slots + slot, tile, fp_here)
                slot += 1
    fp_own[...] = fp_sent
    loads[1].wait()
    pl.semaphore_wait(barrier, len(z_peers) + len(xy_peers) + 1)

    sent = []

    def block(r, m):
        return gathered.at[r, pl.ds(pl.multiple_of(m * md, md), md), :]

    def send(r, m, to):
        copy = pltpu.make_async_remote_copy(
            src_ref=block(r, m),
            dst_ref=block(r, m),
            send_sem=send_sem.at[len(sent)],
            recv_sem=recv_sem.at[r, m],
            device_id=to,
            device_id_type=MESH,
        )
        copy.start()
        sent.append(copy)

    def arrived(r, m):
        pltpu.make_async_remote_copy(
            src_ref=block(r, m),
            dst_ref=block(r, m),
            send_sem=send_sem.at[0],
            recv_sem=recv_sem.at[r, m],
            device_id=(my_r, mate),
            device_id_type=MESH,
        ).wait_recv()

    def fp_copy(i, r_from, r_to):
        return pltpu.make_async_remote_copy(
            src_ref=fp_own,
            dst_ref=fp_all.at[r_from],
            send_sem=fp_send.at[i],
            recv_sem=fp_recv.at[r_from],
            device_id=(r_to, my_m),
            device_id_type=MESH,
        )

    for r in z_peers:
        send(my_r, my_m, (r, my_m))
    for m in xy_peers:
        send(my_r, my_m, (my_r, m))
    send(my_r, my_m, (my_r, mate))
    for i, r in enumerate(z_peers):
        fp_copy(i, my_r, r).start()
    for load in loads[2:]:
        load.wait()

    rows = order_ref.shape[0]
    table = jnp.concatenate(
        [region_ref[...].astype(F32), cell_ref[...].astype(F32)]
        + list(split3(error_ref[...]))
        + list(split3(value_ref[...])),
        axis=0,
    )
    table_t = jnp.transpose(table).astype(BF16)
    width = table.shape[0]
    order_t = jnp.transpose(
        jnp.concatenate([order_ref[...].astype(F32), jnp.zeros((LANES - rows, LANES), F32)], axis=0)
    ).astype(jnp.int32)
    lane = lax.broadcasted_iota(jnp.int32, (LANES, LANES), 1)
    line = lax.broadcasted_iota(jnp.int32, (LANES, LANES), 0)
    wide_lane = lax.broadcasted_iota(jnp.int32, (LANES, width), 1)
    kind = lax.broadcasted_iota(jnp.int32, (width, LANES), 0) // rows
    column = lax.broadcasted_iota(jnp.int32, (width, LANES), 1)
    collect = jnp.where((kind == 0) & (column == 0), float(cd), 0.0)
    collect = jnp.where((kind == 1) & (column == 0), 1.0, collect)
    collect = jnp.where((kind >= 2) & (kind <= 4) & (column == 1), 1.0, collect)
    collect = jnp.where((kind >= 5) & (column == 2), 1.0, collect).astype(BF16)
    for i, r in enumerate(z_peers):
        fp_copy(i, r, r).wait_recv()
        fp_here = fp_here + fp_all[r]
    tile_of = (fp_here + fp_sent)[0:1, :]
    lane1 = lax.broadcasted_iota(jnp.int32, (1, LANES), 1)
    batch_of = lane1 % slots // (tiles_dev * FOOT)
    half = LANES // OTILE
    pick = jnp.where(line == batch_of * (NOBS // LANES) + tile_of // half, 1.0, 0.0).astype(BF16)
    high_all = dot((order_t // LANES).astype(F32).astype(BF16), pick)
    low_all = dot((order_t % LANES).astype(F32).astype(BF16), pick)
    upper = tile_of % half == 1
    high_all = jnp.where(upper, high_all[OTILE:, :], high_all[:OTILE, :]).astype(jnp.int32)
    low_all = jnp.where(upper, low_all[OTILE:, :], low_all[:OTILE, :]).astype(jnp.int32)
    wide = lax.broadcasted_iota(jnp.int32, (LANES, cells), 1)
    firsts = [r * slots + t * FOOT for r in range(nr) for t in range(tiles_dev)]
    firsts += [nr * slots + (tiles_dev + t) * FOOT for t in range(tiles_dev)]
    for q, first in enumerate(firsts):
        here = slice(q * LANES, (q + 1) * LANES)
        high, low = [
            jnp.concatenate([v[:, first + f : first + f + 1] for f in range(FOOT)], axis=0)
            for v in (high_all, low_all)
        ]
        found = dot(jnp.where(lane == low, 1.0, 0.0).astype(BF16), table_t)
        found = jnp.where(wide_lane % rows == high, found, 0.0).astype(BF16)
        found = dot(found, collect)
        feat[here, :] = found
        hot[here, :] = jnp.where(wide == found[:, 0:1].astype(jnp.int32), 1.0, 0.0).astype(BF16)

    for r in z_peers:
        arrived(r, my_m)
        for m in xy_peers:
            send(r, my_m, (my_r, m))
        send(r, my_m, (my_r, mate))
    mate_blocks = [mate] + [((chip + e) % chips) * CORES + (1 - core) for e in range(1, chips)]
    first_obs = nr * tiles_dev * STILE

    def take_in(i, r):
        for m in mate_blocks:
            arrived(r, m)
        here = pl.ds(pl.multiple_of(r * cd, cd), cd)
        turned = jnp.transpose(gathered[r])
        state_t[here, :] = turned
        hi, lo = split2(turned)
        parts[here, :members] = hi
        parts[here, members:] = lo
        mine = hot[:first_obs, here]
        partial = dot(mine, hi) + dot(mine, lo)
        priors[...] = partial if i == 0 else priors[...] + partial

    regions = [my_r] + z_peers
    for i, r in enumerate(regions):
        for m in xy_peers:
            arrived(r, m)
            send(r, m, (my_r, mate))
        if i > 0:
            take_in(i - 1, regions[i - 1])
    take_in(nr - 1, regions[-1])

    firsts = first_obs
    pert, step = obs_terms(priors[...], feat[:firsts, 1:2], feat[:firsts, 2:3], members)
    pert_hi[...], pert_lo[...] = split2(pert)
    step_hi[...], step_lo[...] = split2(step)

    for r in range(nr):
        for t in range(tiles_dev):
            first = r * cd + t * STILE
            obs = slice((r * tiles_dev + t) * STILE, (r * tiles_dev + t + 1) * STILE)
            p_hi, p_lo, s_hi, s_lo = [ref[obs, :] for ref in (pert_hi, pert_lo, step_hi, step_lo)]
            own = (parts[first : first + STILE, :members], parts[first : first + STILE, members:])
            cov = dot3(own, (p_hi, p_lo), transposed=True)
            new = state_t[first : first + STILE, :] + dot3(split2(cov), (s_hi, s_lo))
            state_t[first : first + STILE, :] = new
            hi, lo = split2(new)
            parts[first : first + STILE, :members] = hi
            parts[first : first + STILE, members:] = lo

    for t in range(tiles_dev):
        obs = slice(firsts + t * STILE, firsts + (t + 1) * STILE)
        both = dot(hot[obs, :], parts[...])
        pert, step = obs_terms(
            both[:, :members] + both[:, members:], feat[obs, 1:2], feat[obs, 2:3], members
        )
        here = pl.ds(pl.multiple_of(my_r * cd + t * STILE, STILE), STILE)
        cov = dot3((parts[here, :members], parts[here, members:]), split2(pert), transposed=True)
        new = state_t[here, :] + dot3(split2(cov), split2(step))
        final[:, t * STILE : (t + 1) * STILE] = jnp.transpose(new)
    out_ref[...] = final[pl.ds(pl.multiple_of(my_m * md, md), md), :]

    for copy in sent:
        copy.wait_send()
    for i, r in enumerate(z_peers):
        fp_copy(i, my_r, r).wait_send()


def replicated(nr, nm, ensemble, obs_value, obs_error, obs_region, obs_cell, order, footprint):
    md, cd = ensemble.shape
    members, cells = md * nm, cd * nr
    total = order.shape[0]
    lines = [v.reshape(total // LANES, LANES) for v in (order, obs_region, obs_cell, obs_error, obs_value)]
    line = (total // LANES, LANES)
    chips = nm // CORES
    sends = (nr - 1) + nr * (chips - 1) + nr * chips
    return pl.pallas_call(
        functools.partial(kernel, nr, nm),
        out_shape=jax.ShapeDtypeStruct((md, cd), F32),
        in_specs=[pl.BlockSpec(memory_space=pltpu.HBM)] * 7,
        out_specs=pl.BlockSpec(memory_space=pltpu.VMEM),
        scratch_shapes=[
            pltpu.SMEM(footprint.shape, jnp.int32),
            pltpu.VMEM(line, jnp.int32),
            pltpu.VMEM(line, jnp.int32),
            pltpu.VMEM(line, jnp.int32),
            pltpu.VMEM(line, F32),
            pltpu.VMEM(line, F32),
            pltpu.SemaphoreType.DMA((7,)),
            pltpu.VMEM((nr, members, cd), F32),
            pltpu.VMEM((nr, 8, LANES), jnp.int32),
            pltpu.VMEM((8, LANES), jnp.int32),
            pltpu.VMEM((cells + cd, LANES), F32),
            pltpu.VMEM((cells + cd, cells), BF16),
            pltpu.VMEM((cells, members), F32),
            pltpu.VMEM((cells, members), F32),
            pltpu.VMEM((cells, 2 * members), BF16),
            pltpu.VMEM((cells, members), BF16),
            pltpu.VMEM((cells, members), BF16),
            pltpu.VMEM((cells, members), BF16),
            pltpu.VMEM((cells, members), BF16),
            pltpu.VMEM((members, cd), F32),
            pltpu.SemaphoreType.DMA((sends,)),
            pltpu.SemaphoreType.DMA((nr, nm)),
            pltpu.SemaphoreType.DMA((nr,)),
            pltpu.SemaphoreType.DMA((nr,)),
        ],
        compiler_params=pltpu.CompilerParams(
            collective_id=0, has_side_effects=True, vmem_limit_bytes=64 * 1024 * 1024
        ),
    )(footprint, ensemble, *lines)


def sharded(ensemble, obs_value, obs_error, obs_region, obs_cell, order, footprint):
    mem_dev, cell_count = ensemble.shape
    members = mem_dev * lax.axis_size("member")
    tile_count = cell_count // STILE
    state = ensemble
    region = lax.axis_index("region")
    offsets = jnp.arange(OTILE, dtype=jnp.int32)
    for batch_no in range(BATCHES):
        chosen = order[batch_no * NOBS : (batch_no + 1) * NOBS]
        owned_here = obs_region[chosen] == region
        picked = jnp.where(owned_here[None, :], jnp.take(state, obs_cell[chosen], axis=1), 0.0)
        priors = lax.psum(picked, "region")
        obs_index = (footprint[batch_no][:, :, None] * OTILE + offsets[None, None, :]).reshape(
            tile_count, FOOT * OTILE
        )
        state_tiles = state.reshape(mem_dev, tile_count, STILE)
        s_one = jnp.sum(priors, axis=0)
        s_two = jnp.sum(priors * priors, axis=0)
        s_one, s_two = lax.psum((s_one, s_two), "member")
        obs_mean = s_one / members
        obs_pert = priors - obs_mean[None, :]
        obs_tiles = jnp.take(obs_pert, obs_index, axis=1)
        partial_value = jnp.einsum(
            "mtj,mtc->tjc", obs_tiles, state_tiles, precision=lax.Precision.HIGHEST
        )
        summed = lax.psum(partial_value, "member")
        covariance = summed / (members - 1)
        obs_var = (s_two - s_one * obs_mean) / (members - 1)
        err_var = obs_error[chosen]
        obs_gain = 1.0 / (obs_var + err_var)
        shrink = 1.0 / (1.0 + jnp.sqrt(err_var * obs_gain))
        innovation = obs_value[chosen] - obs_mean
        weight = covariance * obs_gain[obs_index][:, :, None]
        mean_step = jnp.einsum(
            "tjc,tj->tc", weight, innovation[obs_index], precision=lax.Precision.HIGHEST
        )
        scaled = obs_tiles * shrink[obs_index][None, :, :]
        pert_step = jnp.einsum("mtj,tjc->mtc", scaled, weight, precision=lax.Precision.HIGHEST)
        state = (
            state + mean_step.reshape(cell_count)[None, :] - pert_step.reshape(mem_dev, cell_count)
        )
    return state


def solution(mesh):
    nr, nm = mesh.shape["region"], mesh.shape["member"]

    def per_device(ensemble, *rest):
        if 4 * ensemble.size * nr * nm <= REPLICATED_LIMIT:
            return replicated(nr, nm, ensemble, *rest)
        return sharded(ensemble, *rest)

    in_specs = (P("member", "region"), P(), P(), P(), P(), P(), P(None, "region", None))
    out_specs = P("member", "region")
    return jax.shard_map(
        per_device, mesh=mesh, in_specs=in_specs, out_specs=out_specs, check_vma=False
    )
```

```python
import functools

import jax
import jax.numpy as jnp
from jax import lax
from jax.experimental import pallas as pl
from jax.experimental.pallas import tpu as pltpu
from jax.sharding import PartitionSpec as P

NOBS = 1024
BATCHES = 2
STILE = 128
OTILE = 64
FOOT = 2
CORES = 2
LANES = 128
MESH = pl.DeviceIdType.MESH
F32 = jnp.float32
BF16 = jnp.bfloat16
REPLICATED_LIMIT = 4 * 1024 * 1024


def split2(x):
    hi = x.astype(BF16)
    lo = (x - hi.astype(F32)).astype(BF16)
    return hi, lo


def split3(x):
    hi = x.astype(BF16)
    rest = x - hi.astype(F32)
    mid = rest.astype(BF16)
    lo = (rest - mid.astype(F32)).astype(BF16)
    return hi.astype(F32), mid.astype(F32), lo.astype(F32)


def dot(a, b, transposed=False):
    dims = (((1,), (1 if transposed else 0,)), ((), ()))
    return lax.dot_general(a, b, dims, preferred_element_type=F32)


def dot3(a, b, transposed=False):
    a_hi, a_lo = a
    b_hi, b_lo = b
    return dot(a_hi, b_hi, transposed) + (dot(a_hi, b_lo, transposed) + dot(a_lo, b_hi, transposed))


def obs_terms(priors, err, val, members):
    mean = jnp.sum(priors, axis=1, keepdims=True) * (1.0 / members)
    pert = priors - mean
    var = jnp.sum(pert * pert, axis=1, keepdims=True) * (1.0 / (members - 1))
    gain = 1.0 / (var + err)
    shrink = 1.0 / (1.0 + jnp.sqrt(err * gain))
    step = (gain * (1.0 / (members - 1))) * ((val - mean) - shrink * pert)
    return pert, step


def kernel(
    nr, nm, fp_hbm, ens_hbm, order_hbm, region_hbm, cell_hbm, error_hbm, value_hbm, out_ref,
    fp_ref, order_ref, region_ref, cell_ref, error_ref, value_ref, load_sem, gathered, fp_all, fp_own, feat, hot, priors, state_t, parts, pert_hi, pert_lo, step_hi, step_lo, final,
    send_sem, recv_sem, fp_send, fp_recv,
):
    my_r, my_m = lax.axis_index("region"), lax.axis_index("member")
    md, cd = ens_hbm.shape
    members, cells = md * nm, cd * nr
    chips = nm // CORES
    chip, core = my_m // CORES, my_m % CORES
    mate = chip * CORES + (1 - core)
    tiles_dev = cd // STILE
    z_peers = [(my_r + d) % nr for d in sorted(range(1, nr), key=lambda d: min(d, nr - d))]
    xy_peers = [((chip + e) % chips) * CORES + core for e in range(1, chips)]

    own_block = gathered.at[my_r, pl.ds(pl.multiple_of(my_m * md, md), md), :]
    loads = [
        pltpu.make_async_copy(src, dst, load_sem.at[i])
        for i, (src, dst) in enumerate(
            [
                (fp_hbm, fp_ref),
                (ens_hbm, own_block),
                (order_hbm, order_ref),
                (region_hbm, region_ref),
                (cell_hbm, cell_ref),
                (error_hbm, error_ref),
                (value_hbm, value_ref),
            ]
        )
    ]
    for load in loads:
        load.start()
    barrier = pltpu.get_barrier_semaphore()
    for r in z_peers:
        pl.semaphore_signal(barrier, inc=1, device_id=(r, my_m), device_id_type=MESH)
    for m in xy_peers + [mate]:
        pl.semaphore_signal(barrier, inc=1, device_id=(my_r, m), device_id_type=MESH)
    loads[0].wait()
    slots = BATCHES * tiles_dev * FOOT
    lane8 = lax.broadcasted_iota(jnp.int32, (8, LANES), 1)
    fp_sent, fp_here = [jnp.zeros((8, LANES), jnp.int32)] * 2
    slot = 0
    for b in range(BATCHES):
        for t in range(tiles_dev):
            for f in range(FOOT):
                tile = fp_ref[b, t, f]
                fp_sent = jnp.where(lane8 == my_r * slots + slot, tile, fp_sent)
                fp_here = jnp.where(lane8 == nr * slots + slot, tile, fp_here)
                slot += 1
    fp_own[...] = fp_sent
    loads[1].wait()
    pl.semaphore_wait(barrier, len(z_peers) + len(xy_peers) + 1)

    sent = []

    def block(r, m):
        return gathered.at[r, pl.ds(pl.multiple_of(m * md, md), md), :]

    def send(r, m, to):
        copy = pltpu.make_async_remote_copy(
            src_ref=block(r, m),
            dst_ref=block(r, m),
            send_sem=send_sem.at[len(sent)],
            recv_sem=recv_sem.at[r, m],
            device_id=to,
            device_id_type=MESH,
        )
        copy.start()
        sent.append(copy)

    def arrived(r, m):
        pltpu.make_async_remote_copy(
            src_ref=block(r, m),
            dst_ref=block(r, m),
            send_sem=send_sem.at[0],
            recv_sem=recv_sem.at[r, m],
            device_id=(my_r, mate),
            device_id_type=MESH,
        ).wait_recv()

    def fp_copy(i, r_from, r_to):
        return pltpu.make_async_remote_copy(
            src_ref=fp_own,
            dst_ref=fp_all.at[r_from],
            send_sem=fp_send.at[i],
            recv_sem=fp_recv.at[r_from],
            device_id=(r_to, my_m),
            device_id_type=MESH,
        )

    for r in z_peers:
        send(my_r, my_m, (r, my_m))
    for m in xy_peers:
        send(my_r, my_m, (my_r, m))
    send(my_r, my_m, (my_r, mate))
    for i, r in enumerate(z_peers):
        fp_copy(i, my_r, r).start()
    for load in loads[2:]:
        load.wait()

    rows = order_ref.shape[0]
    table = jnp.concatenate(
        [region_ref[...].astype(F32), cell_ref[...].astype(F32)]
        + list(split3(error_ref[...]))
        + list(split3(value_ref[...])),
        axis=0,
    )
    table_t = jnp.transpose(table).astype(BF16)
    width = table.shape[0]
    order_t = jnp.transpose(
        jnp.concatenate([order_ref[...].astype(F32), jnp.zeros((LANES - rows, LANES), F32)], axis=0)
    ).astype(jnp.int32)
    lane = lax.broadcasted_iota(jnp.int32, (LANES, LANES), 1)
    line = lax.broadcasted_iota(jnp.int32, (LANES, LANES), 0)
    wide_lane = lax.broadcasted_iota(jnp.int32, (LANES, width), 1)
    kind = lax.broadcasted_iota(jnp.int32, (width, LANES), 0) // rows
    column = lax.broadcasted_iota(jnp.int32, (width, LANES), 1)
    collect = jnp.where((kind == 0) & (column == 0), float(cd), 0.0)
    collect = jnp.where((kind == 1) & (column == 0), 1.0, collect)
    collect = jnp.where((kind >= 2) & (kind <= 4) & (column == 1), 1.0, collect)
    collect = jnp.where((kind >= 5) & (column == 2), 1.0, collect).astype(BF16)
    for i, r in enumerate(z_peers):
        fp_copy(i, r, r).wait_recv()
        fp_here = fp_here + fp_all[r]
    tile_of = (fp_here + fp_sent)[0:1, :]
    lane1 = lax.broadcasted_iota(jnp.int32, (1, LANES), 1)
    batch_of = lane1 % slots // (tiles_dev * FOOT)
    half = LANES // OTILE
    pick = jnp.where(line == batch_of * (NOBS // LANES) + tile_of // half, 1.0, 0.0).astype(BF16)
    high_all = dot((order_t // LANES).astype(F32).astype(BF16), pick)
    low_all = dot((order_t % LANES).astype(F32).astype(BF16), pick)
    upper = tile_of % half == 1
    high_all = jnp.where(upper, high_all[OTILE:, :], high_all[:OTILE, :]).astype(jnp.int32)
    low_all = jnp.where(upper, low_all[OTILE:, :], low_all[:OTILE, :]).astype(jnp.int32)
    wide = lax.broadcasted_iota(jnp.int32, (LANES, cells), 1)
    firsts = [r * slots + t * FOOT for r in range(nr) for t in range(tiles_dev)]
    firsts += [nr * slots + (tiles_dev + t) * FOOT for t in range(tiles_dev)]
    for q, first in enumerate(firsts):
        here = slice(q * LANES, (q + 1) * LANES)
        high, low = [
            jnp.concatenate([v[:, first + f : first + f + 1] for f in range(FOOT)], axis=0)
            for v in (high_all, low_all)
        ]
        found = dot(jnp.where(lane == low, 1.0, 0.0).astype(BF16), table_t)
        found = jnp.where(wide_lane % rows == high, found, 0.0).astype(BF16)
        found = dot(found, collect)
        feat[here, :] = found
        hot[here, :] = jnp.where(wide == found[:, 0:1].astype(jnp.int32), 1.0, 0.0).astype(BF16)

    for r in z_peers:
        arrived(r, my_m)
        for m in xy_peers:
            send(r, my_m, (my_r, m))
        send(r, my_m, (my_r, mate))
    mate_blocks = [mate] + [((chip + e) % chips) * CORES + (1 - core) for e in range(1, chips)]
    first_obs = nr * tiles_dev * STILE

    def take_in(i, r):
        for m in mate_blocks:
            arrived(r, m)
        here = pl.ds(pl.multiple_of(r * cd, cd), cd)
        turned = jnp.transpose(gathered[r])
        state_t[here, :] = turned
        hi, lo = split2(turned)
        parts[here, :members] = hi
        parts[here, members:] = lo
        mine = hot[:first_obs, here]
        partial = dot(mine, hi) + dot(mine, lo)
        priors[...] = partial if i == 0 else priors[...] + partial

    regions = [my_r] + z_peers
    for i, r in enumerate(regions):
        for m in xy_peers:
            arrived(r, m)
            send(r, m, (my_r, mate))
        if i > 0:
            take_in(i - 1, regions[i - 1])
    take_in(nr - 1, regions[-1])

    firsts = first_obs
    pert, step = obs_terms(priors[...], feat[:firsts, 1:2], feat[:firsts, 2:3], members)
    pert_hi[...], pert_lo[...] = split2(pert)
    step_hi[...], step_lo[...] = split2(step)

    for r in range(nr):
        for t in range(tiles_dev):
            first = r * cd + t * STILE
            obs = slice((r * tiles_dev + t) * STILE, (r * tiles_dev + t + 1) * STILE)
            p_hi, p_lo, s_hi, s_lo = [ref[obs, :] for ref in (pert_hi, pert_lo, step_hi, step_lo)]
            own = (parts[first : first + STILE, :members], parts[first : first + STILE, members:])
            cov = dot3(own, (p_hi, p_lo), transposed=True)
            new = state_t[first : first + STILE, :] + dot3(split2(cov), (s_hi, s_lo))
            state_t[first : first + STILE, :] = new
            hi, lo = split2(new)
            parts[first : first + STILE, :members] = hi
            parts[first : first + STILE, members:] = lo

    for t in range(tiles_dev):
        obs = slice(firsts + t * STILE, firsts + (t + 1) * STILE)
        both = dot(hot[obs, :], parts[...])
        pert, step = obs_terms(
            both[:, :members] + both[:, members:], feat[obs, 1:2], feat[obs, 2:3], members
        )
        here = pl.ds(pl.multiple_of(my_r * cd + t * STILE, STILE), STILE)
        cov = dot3((parts[here, :members], parts[here, members:]), split2(pert), transposed=True)
        new = state_t[here, :] + dot3(split2(cov), split2(step))
        final[:, t * STILE : (t + 1) * STILE] = jnp.transpose(new)
    out_ref[...] = final[pl.ds(pl.multiple_of(my_m * md, md), md), :]

    for copy in sent:
        copy.wait_send()
    for i, r in enumerate(z_peers):
        fp_copy(i, my_r, r).wait_send()


def replicated(nr, nm, ensemble, obs_value, obs_error, obs_region, obs_cell, order, footprint):
    md, cd = ensemble.shape
    members, cells = md * nm, cd * nr
    total = order.shape[0]
    lines = [v.reshape(total // LANES, LANES) for v in (order, obs_region, obs_cell, obs_error, obs_value)]
    line = (total // LANES, LANES)
    chips = nm // CORES
    sends = (nr - 1) + nr * (chips - 1) + nr * chips
    return pl.pallas_call(
        functools.partial(kernel, nr, nm),
        out_shape=jax.ShapeDtypeStruct((md, cd), F32),
        in_specs=[pl.BlockSpec(memory_space=pltpu.HBM)] * 7,
        out_specs=pl.BlockSpec(memory_space=pltpu.VMEM),
        scratch_shapes=[
            pltpu.SMEM(footprint.shape, jnp.int32),
            pltpu.VMEM(line, jnp.int32),
            pltpu.VMEM(line, jnp.int32),
            pltpu.VMEM(line, jnp.int32),
            pltpu.VMEM(line, F32),
            pltpu.VMEM(line, F32),
            pltpu.SemaphoreType.DMA((7,)),
            pltpu.VMEM((nr, members, cd), F32),
            pltpu.VMEM((nr, 8, LANES), jnp.int32),
            pltpu.VMEM((8, LANES), jnp.int32),
            pltpu.VMEM((cells + cd, LANES), F32),
            pltpu.VMEM((cells + cd, cells), BF16),
            pltpu.VMEM((cells, members), F32),
            pltpu.VMEM((cells, members), F32),
            pltpu.VMEM((cells, 2 * members), BF16),
            pltpu.VMEM((cells, members), BF16),
            pltpu.VMEM((cells, members), BF16),
            pltpu.VMEM((cells, members), BF16),
            pltpu.VMEM((cells, members), BF16),
            pltpu.VMEM((members, cd), F32),
            pltpu.SemaphoreType.DMA((sends,)),
            pltpu.SemaphoreType.DMA((nr, nm)),
            pltpu.SemaphoreType.DMA((nr,)),
            pltpu.SemaphoreType.DMA((nr,)),
        ],
        compiler_params=pltpu.CompilerParams(
            collective_id=0, has_side_effects=True, vmem_limit_bytes=48 * 1024 * 1024
        ),
    )(*[pltpu.with_memory_space_constraint(v, pltpu.HBM) for v in (footprint, ensemble, *lines)])


def sharded(ensemble, obs_value, obs_error, obs_region, obs_cell, order, footprint):
    mem_dev, cell_count = ensemble.shape
    members = mem_dev * lax.axis_size("member")
    tile_count = cell_count // STILE
    state = ensemble
    region = lax.axis_index("region")
    offsets = jnp.arange(OTILE, dtype=jnp.int32)
    for batch_no in range(BATCHES):
        chosen = order[batch_no * NOBS : (batch_no + 1) * NOBS]
        owned_here = obs_region[chosen] == region
        picked = jnp.where(owned_here[None, :], jnp.take(state, obs_cell[chosen], axis=1), 0.0)
        priors = lax.psum(picked, "region")
        obs_index = (footprint[batch_no][:, :, None] * OTILE + offsets[None, None, :]).reshape(
            tile_count, FOOT * OTILE
        )
        state_tiles = state.reshape(mem_dev, tile_count, STILE)
        s_one = jnp.sum(priors, axis=0)
        s_two = jnp.sum(priors * priors, axis=0)
        s_one, s_two = lax.psum((s_one, s_two), "member")
        obs_mean = s_one / members
        obs_pert = priors - obs_mean[None, :]
        obs_tiles = jnp.take(obs_pert, obs_index, axis=1)
        partial_value = jnp.einsum(
            "mtj,mtc->tjc", obs_tiles, state_tiles, precision=lax.Precision.HIGHEST
        )
        summed = lax.psum(partial_value, "member")
        covariance = summed / (members - 1)
        obs_var = (s_two - s_one * obs_mean) / (members - 1)
        err_var = obs_error[chosen]
        obs_gain = 1.0 / (obs_var + err_var)
        shrink = 1.0 / (1.0 + jnp.sqrt(err_var * obs_gain))
        innovation = obs_value[chosen] - obs_mean
        weight = covariance * obs_gain[obs_index][:, :, None]
        mean_step = jnp.einsum(
            "tjc,tj->tc", weight, innovation[obs_index], precision=lax.Precision.HIGHEST
        )
        scaled = obs_tiles * shrink[obs_index][None, :, :]
        pert_step = jnp.einsum("mtj,tjc->mtc", scaled, weight, precision=lax.Precision.HIGHEST)
        state = (
            state + mean_step.reshape(cell_count)[None, :] - pert_step.reshape(mem_dev, cell_count)
        )
    return state


def solution(mesh):
    nr, nm = mesh.shape["region"], mesh.shape["member"]

    def per_device(ensemble, *rest):
        if 4 * ensemble.size * nr * nm <= REPLICATED_LIMIT:
            return replicated(nr, nm, ensemble, *rest)
        return sharded(ensemble, *rest)

    in_specs = (P("member", "region"), P(), P(), P(), P(), P(), P(None, "region", None))
    out_specs = P("member", "region")
    return jax.shard_map(
        per_device, mesh=mesh, in_specs=in_specs, out_specs=out_specs, check_vma=False
    )
```

```python
import functools

import jax
import jax.numpy as jnp
from jax import lax
from jax.experimental import pallas as pl
from jax.experimental.pallas import tpu as pltpu
from jax.sharding import PartitionSpec as P

NOBS = 1024
BATCHES = 2
STILE = 128
OTILE = 64
FOOT = 2
CORES = 2
LANES = 128
MESH = pl.DeviceIdType.MESH
F32 = jnp.float32
BF16 = jnp.bfloat16
REPLICATED_LIMIT = 4 * 1024 * 1024


def split2(x):
    hi = x.astype(BF16)
    lo = (x - hi.astype(F32)).astype(BF16)
    return hi, lo


def split3(x):
    hi = x.astype(BF16)
    rest = x - hi.astype(F32)
    mid = rest.astype(BF16)
    lo = (rest - mid.astype(F32)).astype(BF16)
    return hi.astype(F32), mid.astype(F32), lo.astype(F32)


def dot(a, b, transposed=False):
    dims = (((1,), (1 if transposed else 0,)), ((), ()))
    return lax.dot_general(a, b, dims, preferred_element_type=F32)


def dot3(a, b, transposed=False):
    a_hi, a_lo = a
    b_hi, b_lo = b
    return dot(a_hi, b_hi, transposed) + (dot(a_hi, b_lo, transposed) + dot(a_lo, b_hi, transposed))


def obs_terms(priors, err, val, err_root, members):
    mean = jnp.sum(priors, axis=1, keepdims=True) * (1.0 / members)
    pert = priors - mean
    var = jnp.sum(pert * pert, axis=1, keepdims=True) * (1.0 / (members - 1))
    root = lax.rsqrt(var + err)
    gain = root * root
    shrink = 1.0 / (1.0 + err_root * root)
    step = (gain * (1.0 / (members - 1))) * ((val - mean) - shrink * pert)
    return pert, step


def kernel(
    nr, nm, fp_hbm, ens_hbm, order_hbm, region_hbm, cell_hbm, error_hbm, value_hbm, out_ref,
    fp_ref, order_ref, region_ref, cell_ref, error_ref, value_ref, load_sem, gathered, fp_all, fp_own, feat, hot, priors, state_t, parts, pert_hi, pert_lo, step_hi, step_lo, final,
    send_sem, recv_sem, fp_send, fp_recv,
):
    my_r, my_m = lax.axis_index("region"), lax.axis_index("member")
    md, cd = ens_hbm.shape
    members, cells = md * nm, cd * nr
    chips = nm // CORES
    chip, core = my_m // CORES, my_m % CORES
    mate = chip * CORES + (1 - core)
    tiles_dev = cd // STILE
    z_peers = [(my_r + d) % nr for d in sorted(range(1, nr), key=lambda d: min(d, nr - d))]
    xy_peers = [((chip + e) % chips) * CORES + core for e in range(1, chips)]

    own_block = gathered.at[my_r, pl.ds(pl.multiple_of(my_m * md, md), md), :]
    loads = [
        pltpu.make_async_copy(src, dst, load_sem.at[i])
        for i, (src, dst) in enumerate(
            [
                (fp_hbm, fp_ref),
                (ens_hbm, own_block),
                (order_hbm, order_ref),
                (region_hbm, region_ref),
                (cell_hbm, cell_ref),
                (error_hbm, error_ref),
                (value_hbm, value_ref),
            ]
        )
    ]
    for load in loads:
        load.start()
    barrier = pltpu.get_barrier_semaphore()
    for r in z_peers:
        pl.semaphore_signal(barrier, inc=1, device_id=(r, my_m), device_id_type=MESH)
    for m in xy_peers + [mate]:
        pl.semaphore_signal(barrier, inc=1, device_id=(my_r, m), device_id_type=MESH)
    loads[0].wait()
    slots = BATCHES * tiles_dev * FOOT
    lane8 = lax.broadcasted_iota(jnp.int32, (8, LANES), 1)
    fp_sent, fp_here = [jnp.zeros((8, LANES), jnp.int32)] * 2
    slot = 0
    for b in range(BATCHES):
        for t in range(tiles_dev):
            for f in range(FOOT):
                tile = fp_ref[b, t, f]
                fp_sent = jnp.where(lane8 == my_r * slots + slot, tile, fp_sent)
                fp_here = jnp.where(lane8 == nr * slots + slot, tile, fp_here)
                slot += 1
    fp_own[...] = fp_sent
    loads[1].wait()
    pl.semaphore_wait(barrier, len(z_peers) + len(xy_peers) + 1)

    sent = []

    def block(r, m):
        return gathered.at[r, pl.ds(pl.multiple_of(m * md, md), md), :]

    def send(r, m, to):
        copy = pltpu.make_async_remote_copy(
            src_ref=block(r, m),
            dst_ref=block(r, m),
            send_sem=send_sem.at[len(sent)],
            recv_sem=recv_sem.at[r, m],
            device_id=to,
            device_id_type=MESH,
        )
        copy.start()
        sent.append(copy)

    def arrived(r, m):
        pltpu.make_async_remote_copy(
            src_ref=block(r, m),
            dst_ref=block(r, m),
            send_sem=send_sem.at[0],
            recv_sem=recv_sem.at[r, m],
            device_id=(my_r, mate),
            device_id_type=MESH,
        ).wait_recv()

    def fp_copy(i, r_from, r_to):
        return pltpu.make_async_remote_copy(
            src_ref=fp_own,
            dst_ref=fp_all.at[r_from],
            send_sem=fp_send.at[i],
            recv_sem=fp_recv.at[r_from],
            device_id=(r_to, my_m),
            device_id_type=MESH,
        )

    for r in z_peers:
        send(my_r, my_m, (r, my_m))
    for m in xy_peers:
        send(my_r, my_m, (my_r, m))
    send(my_r, my_m, (my_r, mate))
    for i, r in enumerate(z_peers):
        fp_copy(i, my_r, r).start()
    for load in loads[2:]:
        load.wait()

    rows = order_ref.shape[0]
    table = jnp.concatenate(
        [region_ref[...].astype(F32), cell_ref[...].astype(F32)]
        + list(split3(error_ref[...]))
        + list(split3(value_ref[...])),
        axis=0,
    )
    table_t = jnp.transpose(table).astype(BF16)
    width = table.shape[0]
    order_t = jnp.transpose(
        jnp.concatenate([order_ref[...].astype(F32), jnp.zeros((LANES - rows, LANES), F32)], axis=0)
    ).astype(jnp.int32)
    lane = lax.broadcasted_iota(jnp.int32, (LANES, LANES), 1)
    line = lax.broadcasted_iota(jnp.int32, (LANES, LANES), 0)
    wide_lane = lax.broadcasted_iota(jnp.int32, (LANES, width), 1)
    kind = lax.broadcasted_iota(jnp.int32, (width, LANES), 0) // rows
    column = lax.broadcasted_iota(jnp.int32, (width, LANES), 1)
    collect = jnp.where((kind == 0) & (column == 0), float(cd), 0.0)
    collect = jnp.where((kind == 1) & (column == 0), 1.0, collect)
    collect = jnp.where((kind >= 2) & (kind <= 4) & (column == 1), 1.0, collect)
    collect = jnp.where((kind >= 5) & (column == 2), 1.0, collect).astype(BF16)
    for i, r in enumerate(z_peers):
        fp_copy(i, r, r).wait_recv()
        fp_here = fp_here + fp_all[r]
    tile_of = (fp_here + fp_sent)[0:1, :]
    lane1 = lax.broadcasted_iota(jnp.int32, (1, LANES), 1)
    batch_of = lane1 % slots // (tiles_dev * FOOT)
    half = LANES // OTILE
    pick = jnp.where(line == batch_of * (NOBS // LANES) + tile_of // half, 1.0, 0.0).astype(BF16)
    high_all = dot((order_t // LANES).astype(F32).astype(BF16), pick)
    low_all = dot((order_t % LANES).astype(F32).astype(BF16), pick)
    upper = tile_of % half == 1
    high_all = jnp.where(upper, high_all[OTILE:, :], high_all[:OTILE, :]).astype(jnp.int32)
    low_all = jnp.where(upper, low_all[OTILE:, :], low_all[:OTILE, :]).astype(jnp.int32)
    wide = lax.broadcasted_iota(jnp.int32, (LANES, cells), 1)
    firsts = [r * slots + t * FOOT for r in range(nr) for t in range(tiles_dev)]
    firsts += [nr * slots + (tiles_dev + t) * FOOT for t in range(tiles_dev)]
    for q, first in enumerate(firsts):
        here = slice(q * LANES, (q + 1) * LANES)
        high, low = [
            jnp.concatenate([v[:, first + f : first + f + 1] for f in range(FOOT)], axis=0)
            for v in (high_all, low_all)
        ]
        found = dot(jnp.where(lane == low, 1.0, 0.0).astype(BF16), table_t)
        found = jnp.where(wide_lane % rows == high, found, 0.0).astype(BF16)
        found = dot(found, collect)
        feat[here, :] = jnp.where(lane == 3, jnp.sqrt(found[:, 1:2]), found)
        hot[here, :] = jnp.where(wide == found[:, 0:1].astype(jnp.int32), 1.0, 0.0).astype(BF16)

    for r in z_peers:
        arrived(r, my_m)
        for m in xy_peers:
            send(r, my_m, (my_r, m))
        send(r, my_m, (my_r, mate))
    mate_blocks = [mate] + [((chip + e) % chips) * CORES + (1 - core) for e in range(1, chips)]
    first_obs = nr * tiles_dev * STILE

    def take_in(i, r):
        for m in mate_blocks:
            arrived(r, m)
        here = pl.ds(pl.multiple_of(r * cd, cd), cd)
        turned = jnp.transpose(gathered[r])
        state_t[here, :] = turned
        hi, lo = split2(turned)
        parts[here, :members] = hi
        parts[here, members:] = lo
        mine = hot[:first_obs, here]
        partial = dot(mine, hi) + dot(mine, lo)
        priors[...] = partial if i == 0 else priors[...] + partial

    regions = [my_r] + z_peers
    for i, r in enumerate(regions):
        for m in xy_peers:
            arrived(r, m)
            send(r, m, (my_r, mate))
        if i > 0:
            take_in(i - 1, regions[i - 1])
    take_in(nr - 1, regions[-1])

    firsts = first_obs
    pert, step = obs_terms(priors[...], feat[:firsts, 1:2], feat[:firsts, 2:3], feat[:firsts, 3:4], members)
    pert_hi[...], pert_lo[...] = split2(pert)
    step_hi[...], step_lo[...] = split2(step)

    for r in range(nr):
        for t in range(tiles_dev):
            first = r * cd + t * STILE
            obs = slice((r * tiles_dev + t) * STILE, (r * tiles_dev + t + 1) * STILE)
            p_hi, p_lo, s_hi, s_lo = [ref[obs, :] for ref in (pert_hi, pert_lo, step_hi, step_lo)]
            own = (parts[first : first + STILE, :members], parts[first : first + STILE, members:])
            cov = dot3(own, (p_hi, p_lo), transposed=True)
            new = state_t[first : first + STILE, :] + dot3(split2(cov), (s_hi, s_lo))
            state_t[first : first + STILE, :] = new
            hi, lo = split2(new)
            parts[first : first + STILE, :members] = hi
            parts[first : first + STILE, members:] = lo

    for t in range(tiles_dev):
        obs = slice(firsts + t * STILE, firsts + (t + 1) * STILE)
        both = dot(hot[obs, :], parts[...])
        pert, step = obs_terms(
            both[:, :members] + both[:, members:], feat[obs, 1:2], feat[obs, 2:3], feat[obs, 3:4], members
        )
        here = pl.ds(pl.multiple_of(my_r * cd + t * STILE, STILE), STILE)
        cov = dot3((parts[here, :members], parts[here, members:]), split2(pert), transposed=True)
        new = state_t[here, :] + dot3(split2(cov), split2(step))
        final[:, t * STILE : (t + 1) * STILE] = jnp.transpose(new)
    out_ref[...] = final[pl.ds(pl.multiple_of(my_m * md, md), md), :]

    for copy in sent:
        copy.wait_send()
    for i, r in enumerate(z_peers):
        fp_copy(i, my_r, r).wait_send()


def replicated(nr, nm, ensemble, obs_value, obs_error, obs_region, obs_cell, order, footprint):
    md, cd = ensemble.shape
    members, cells = md * nm, cd * nr
    total = order.shape[0]
    lines = [v.reshape(total // LANES, LANES) for v in (order, obs_region, obs_cell, obs_error, obs_value)]
    line = (total // LANES, LANES)
    chips = nm // CORES
    sends = (nr - 1) + nr * (chips - 1) + nr * chips
    return pl.pallas_call(
        functools.partial(kernel, nr, nm),
        out_shape=jax.ShapeDtypeStruct((md, cd), F32),
        in_specs=[pl.BlockSpec(memory_space=pltpu.HBM)] * 7,
        out_specs=pl.BlockSpec(memory_space=pltpu.VMEM),
        scratch_shapes=[
            pltpu.SMEM(footprint.shape, jnp.int32),
            pltpu.VMEM(line, jnp.int32),
            pltpu.VMEM(line, jnp.int32),
            pltpu.VMEM(line, jnp.int32),
            pltpu.VMEM(line, F32),
            pltpu.VMEM(line, F32),
            pltpu.SemaphoreType.DMA((7,)),
            pltpu.VMEM((nr, members, cd), F32),
            pltpu.VMEM((nr, 8, LANES), jnp.int32),
            pltpu.VMEM((8, LANES), jnp.int32),
            pltpu.VMEM((cells + cd, LANES), F32),
            pltpu.VMEM((cells + cd, cells), BF16),
            pltpu.VMEM((cells, members), F32),
            pltpu.VMEM((cells, members), F32),
            pltpu.VMEM((cells, 2 * members), BF16),
            pltpu.VMEM((cells, members), BF16),
            pltpu.VMEM((cells, members), BF16),
            pltpu.VMEM((cells, members), BF16),
            pltpu.VMEM((cells, members), BF16),
            pltpu.VMEM((members, cd), F32),
            pltpu.SemaphoreType.DMA((sends,)),
            pltpu.SemaphoreType.DMA((nr, nm)),
            pltpu.SemaphoreType.DMA((nr,)),
            pltpu.SemaphoreType.DMA((nr,)),
        ],
        compiler_params=pltpu.CompilerParams(
            collective_id=0, has_side_effects=True, vmem_limit_bytes=48 * 1024 * 1024
        ),
    )(*[pltpu.with_memory_space_constraint(v, pltpu.HBM) for v in (footprint, ensemble, *lines)])


def sharded(ensemble, obs_value, obs_error, obs_region, obs_cell, order, footprint):
    mem_dev, cell_count = ensemble.shape
    members = mem_dev * lax.axis_size("member")
    tile_count = cell_count // STILE
    state = ensemble
    region = lax.axis_index("region")
    offsets = jnp.arange(OTILE, dtype=jnp.int32)
    for batch_no in range(BATCHES):
        chosen = order[batch_no * NOBS : (batch_no + 1) * NOBS]
        owned_here = obs_region[chosen] == region
        picked = jnp.where(owned_here[None, :], jnp.take(state, obs_cell[chosen], axis=1), 0.0)
        priors = lax.psum(picked, "region")
        obs_index = (footprint[batch_no][:, :, None] * OTILE + offsets[None, None, :]).reshape(
            tile_count, FOOT * OTILE
        )
        state_tiles = state.reshape(mem_dev, tile_count, STILE)
        s_one = jnp.sum(priors, axis=0)
        s_two = jnp.sum(priors * priors, axis=0)
        s_one, s_two = lax.psum((s_one, s_two), "member")
        obs_mean = s_one / members
        obs_pert = priors - obs_mean[None, :]
        obs_tiles = jnp.take(obs_pert, obs_index, axis=1)
        partial_value = jnp.einsum(
            "mtj,mtc->tjc", obs_tiles, state_tiles, precision=lax.Precision.HIGHEST
        )
        summed = lax.psum(partial_value, "member")
        covariance = summed / (members - 1)
        obs_var = (s_two - s_one * obs_mean) / (members - 1)
        err_var = obs_error[chosen]
        obs_gain = 1.0 / (obs_var + err_var)
        shrink = 1.0 / (1.0 + jnp.sqrt(err_var * obs_gain))
        innovation = obs_value[chosen] - obs_mean
        weight = covariance * obs_gain[obs_index][:, :, None]
        mean_step = jnp.einsum(
            "tjc,tj->tc", weight, innovation[obs_index], precision=lax.Precision.HIGHEST
        )
        scaled = obs_tiles * shrink[obs_index][None, :, :]
        pert_step = jnp.einsum("mtj,tjc->mtc", scaled, weight, precision=lax.Precision.HIGHEST)
        state = (
            state + mean_step.reshape(cell_count)[None, :] - pert_step.reshape(mem_dev, cell_count)
        )
    return state


def solution(mesh):
    nr, nm = mesh.shape["region"], mesh.shape["member"]

    def per_device(ensemble, *rest):
        if 4 * ensemble.size * nr * nm <= REPLICATED_LIMIT:
            return replicated(nr, nm, ensemble, *rest)
        return sharded(ensemble, *rest)

    in_specs = (P("member", "region"), P(), P(), P(), P(), P(), P(None, "region", None))
    out_specs = P("member", "region")
    return jax.shard_map(
        per_device, mesh=mesh, in_specs=in_specs, out_specs=out_specs, check_vma=False
    )
```

```python
import functools

import jax
import jax.numpy as jnp
from jax import lax
from jax.experimental import pallas as pl
from jax.experimental.pallas import tpu as pltpu
from jax.sharding import PartitionSpec as P

NOBS = 1024
BATCHES = 2
STILE = 128
OTILE = 64
FOOT = 2
CORES = 2
LANES = 128
MESH = pl.DeviceIdType.MESH
F32 = jnp.float32
BF16 = jnp.bfloat16
REPLICATED_LIMIT = 4 * 1024 * 1024


def split2(x):
    hi = x.astype(BF16)
    lo = (x - hi.astype(F32)).astype(BF16)
    return hi, lo


def split3(x):
    hi = x.astype(BF16)
    rest = x - hi.astype(F32)
    mid = rest.astype(BF16)
    lo = (rest - mid.astype(F32)).astype(BF16)
    return hi.astype(F32), mid.astype(F32), lo.astype(F32)


def dot(a, b, transposed=False):
    dims = (((1,), (1 if transposed else 0,)), ((), ()))
    return lax.dot_general(a, b, dims, preferred_element_type=F32)


def dot3(a, b, transposed=False):
    a_hi, a_lo = a
    b_hi, b_lo = b
    left = jnp.concatenate([a_hi, a_hi, a_lo], axis=1)
    right = jnp.concatenate([b_hi, b_lo, b_hi], axis=1 if transposed else 0)
    return dot(left, right, transposed)


def obs_terms(priors, err, val, members):
    mean = jnp.sum(priors, axis=1, keepdims=True) * (1.0 / members)
    pert = priors - mean
    var = jnp.sum(pert * pert, axis=1, keepdims=True) * (1.0 / (members - 1))
    gain = 1.0 / (var + err)
    shrink = 1.0 / (1.0 + jnp.sqrt(err * gain))
    step = (gain * (1.0 / (members - 1))) * ((val - mean) - shrink * pert)
    return pert, step


def kernel(
    nr, nm, fp_hbm, ens_hbm, order_hbm, region_hbm, cell_hbm, error_hbm, value_hbm, out_ref,
    fp_ref, order_ref, region_ref, cell_ref, error_ref, value_ref, load_sem, gathered, fp_all, fp_own, feat, hot, priors, state_t, parts, pert_hi, pert_lo, step_hi, step_lo, final,
    send_sem, recv_sem, fp_send, fp_recv,
):
    my_r, my_m = lax.axis_index("region"), lax.axis_index("member")
    md, cd = ens_hbm.shape
    members, cells = md * nm, cd * nr
    chips = nm // CORES
    chip, core = my_m // CORES, my_m % CORES
    mate = chip * CORES + (1 - core)
    tiles_dev = cd // STILE
    z_peers = [(my_r + d) % nr for d in sorted(range(1, nr), key=lambda d: min(d, nr - d))]
    xy_peers = [((chip + e) % chips) * CORES + core for e in range(1, chips)]

    own_block = gathered.at[my_r, pl.ds(pl.multiple_of(my_m * md, md), md), :]
    loads = [
        pltpu.make_async_copy(src, dst, load_sem.at[i])
        for i, (src, dst) in enumerate(
            [
                (fp_hbm, fp_ref),
                (ens_hbm, own_block),
                (order_hbm, order_ref),
                (region_hbm, region_ref),
                (cell_hbm, cell_ref),
                (error_hbm, error_ref),
                (value_hbm, value_ref),
            ]
        )
    ]
    for load in loads:
        load.start()
    barrier = pltpu.get_barrier_semaphore()
    for r in z_peers:
        pl.semaphore_signal(barrier, inc=1, device_id=(r, my_m), device_id_type=MESH)
    for m in xy_peers + [mate]:
        pl.semaphore_signal(barrier, inc=1, device_id=(my_r, m), device_id_type=MESH)
    loads[0].wait()
    slots = BATCHES * tiles_dev * FOOT
    lane8 = lax.broadcasted_iota(jnp.int32, (8, LANES), 1)
    fp_sent, fp_here = [jnp.zeros((8, LANES), jnp.int32)] * 2
    slot = 0
    for b in range(BATCHES):
        for t in range(tiles_dev):
            for f in range(FOOT):
                tile = fp_ref[b, t, f]
                fp_sent = jnp.where(lane8 == my_r * slots + slot, tile, fp_sent)
                fp_here = jnp.where(lane8 == nr * slots + slot, tile, fp_here)
                slot += 1
    fp_own[...] = fp_sent
    loads[1].wait()
    pl.semaphore_wait(barrier, len(z_peers) + len(xy_peers) + 1)

    sent = []

    def block(r, m):
        return gathered.at[r, pl.ds(pl.multiple_of(m * md, md), md), :]

    def send(r, m, to):
        copy = pltpu.make_async_remote_copy(
            src_ref=block(r, m),
            dst_ref=block(r, m),
            send_sem=send_sem.at[len(sent)],
            recv_sem=recv_sem.at[r, m],
            device_id=to,
            device_id_type=MESH,
        )
        copy.start()
        sent.append(copy)

    def arrived(r, m):
        pltpu.make_async_remote_copy(
            src_ref=block(r, m),
            dst_ref=block(r, m),
            send_sem=send_sem.at[0],
            recv_sem=recv_sem.at[r, m],
            device_id=(my_r, mate),
            device_id_type=MESH,
        ).wait_recv()

    def fp_copy(i, r_from, r_to):
        return pltpu.make_async_remote_copy(
            src_ref=fp_own,
            dst_ref=fp_all.at[r_from],
            send_sem=fp_send.at[i],
            recv_sem=fp_recv.at[r_from],
            device_id=(r_to, my_m),
            device_id_type=MESH,
        )

    for r in z_peers:
        send(my_r, my_m, (r, my_m))
    for m in xy_peers:
        send(my_r, my_m, (my_r, m))
    send(my_r, my_m, (my_r, mate))
    for i, r in enumerate(z_peers):
        fp_copy(i, my_r, r).start()
    for load in loads[2:]:
        load.wait()

    rows = order_ref.shape[0]
    table = jnp.concatenate(
        [region_ref[...].astype(F32), cell_ref[...].astype(F32)]
        + list(split3(error_ref[...]))
        + list(split3(value_ref[...])),
        axis=0,
    )
    table_t = jnp.transpose(table).astype(BF16)
    width = table.shape[0]
    order_t = jnp.transpose(
        jnp.concatenate([order_ref[...].astype(F32), jnp.zeros((LANES - rows, LANES), F32)], axis=0)
    ).astype(jnp.int32)
    lane = lax.broadcasted_iota(jnp.int32, (LANES, LANES), 1)
    line = lax.broadcasted_iota(jnp.int32, (LANES, LANES), 0)
    wide_lane = lax.broadcasted_iota(jnp.int32, (LANES, width), 1)
    kind = lax.broadcasted_iota(jnp.int32, (width, LANES), 0) // rows
    column = lax.broadcasted_iota(jnp.int32, (width, LANES), 1)
    collect = jnp.where((kind == 0) & (column == 0), float(cd), 0.0)
    collect = jnp.where((kind == 1) & (column == 0), 1.0, collect)
    collect = jnp.where((kind >= 2) & (kind <= 4) & (column == 1), 1.0, collect)
    collect = jnp.where((kind >= 5) & (column == 2), 1.0, collect).astype(BF16)
    for i, r in enumerate(z_peers):
        fp_copy(i, r, r).wait_recv()
        fp_here = fp_here + fp_all[r]
    tile_of = (fp_here + fp_sent)[0:1, :]
    lane1 = lax.broadcasted_iota(jnp.int32, (1, LANES), 1)
    batch_of = lane1 % slots // (tiles_dev * FOOT)
    half = LANES // OTILE
    pick = jnp.where(line == batch_of * (NOBS // LANES) + tile_of // half, 1.0, 0.0).astype(BF16)
    high_all = dot((order_t // LANES).astype(F32).astype(BF16), pick)
    low_all = dot((order_t % LANES).astype(F32).astype(BF16), pick)
    upper = tile_of % half == 1
    high_all = jnp.where(upper, high_all[OTILE:, :], high_all[:OTILE, :]).astype(jnp.int32)
    low_all = jnp.where(upper, low_all[OTILE:, :], low_all[:OTILE, :]).astype(jnp.int32)
    wide = lax.broadcasted_iota(jnp.int32, (LANES, cells), 1)
    firsts = [r * slots + t * FOOT for r in range(nr) for t in range(tiles_dev)]
    firsts += [nr * slots + (tiles_dev + t) * FOOT for t in range(tiles_dev)]
    for q, first in enumerate(firsts):
        here = slice(q * LANES, (q + 1) * LANES)
        high, low = [
            jnp.concatenate([v[:, first + f : first + f + 1] for f in range(FOOT)], axis=0)
            for v in (high_all, low_all)
        ]
        found = dot(jnp.where(lane == low, 1.0, 0.0).astype(BF16), table_t)
        found = jnp.where(wide_lane % rows == high, found, 0.0).astype(BF16)
        found = dot(found, collect)
        feat[here, :] = found
        hot[here, :] = jnp.where(wide == found[:, 0:1].astype(jnp.int32), 1.0, 0.0).astype(BF16)

    for r in z_peers:
        arrived(r, my_m)
        for m in xy_peers:
            send(r, my_m, (my_r, m))
        send(r, my_m, (my_r, mate))
    mate_blocks = [mate] + [((chip + e) % chips) * CORES + (1 - core) for e in range(1, chips)]
    first_obs = nr * tiles_dev * STILE

    def take_in(i, r):
        for m in mate_blocks:
            arrived(r, m)
        here = pl.ds(pl.multiple_of(r * cd, cd), cd)
        turned = jnp.transpose(gathered[r])
        state_t[here, :] = turned
        hi, lo = split2(turned)
        parts[here, :members] = hi
        parts[here, members:] = lo
        mine = hot[:first_obs, here]
        partial = dot(mine, hi) + dot(mine, lo)
        priors[...] = partial if i == 0 else priors[...] + partial

    regions = [my_r] + z_peers
    for i, r in enumerate(regions):
        for m in xy_peers:
            arrived(r, m)
            send(r, m, (my_r, mate))
        if i > 0:
            take_in(i - 1, regions[i - 1])
    take_in(nr - 1, regions[-1])

    firsts = first_obs
    pert, step = obs_terms(priors[...], feat[:firsts, 1:2], feat[:firsts, 2:3], members)
    pert_hi[...], pert_lo[...] = split2(pert)
    step_hi[...], step_lo[...] = split2(step)

    for r in range(nr):
        for t in range(tiles_dev):
            first = r * cd + t * STILE
            obs = slice((r * tiles_dev + t) * STILE, (r * tiles_dev + t + 1) * STILE)
            p_hi, p_lo, s_hi, s_lo = [ref[obs, :] for ref in (pert_hi, pert_lo, step_hi, step_lo)]
            own = (parts[first : first + STILE, :members], parts[first : first + STILE, members:])
            cov = dot3(own, (p_hi, p_lo), transposed=True)
            new = state_t[first : first + STILE, :] + dot3(split2(cov), (s_hi, s_lo))
            state_t[first : first + STILE, :] = new
            hi, lo = split2(new)
            parts[first : first + STILE, :members] = hi
            parts[first : first + STILE, members:] = lo

    for t in range(tiles_dev):
        obs = slice(firsts + t * STILE, firsts + (t + 1) * STILE)
        both = dot(hot[obs, :], parts[...])
        pert, step = obs_terms(
            both[:, :members] + both[:, members:], feat[obs, 1:2], feat[obs, 2:3], members
        )
        here = pl.ds(pl.multiple_of(my_r * cd + t * STILE, STILE), STILE)
        cov = dot3((parts[here, :members], parts[here, members:]), split2(pert), transposed=True)
        new = state_t[here, :] + dot3(split2(cov), split2(step))
        final[:, t * STILE : (t + 1) * STILE] = jnp.transpose(new)
    out_ref[...] = final[pl.ds(pl.multiple_of(my_m * md, md), md), :]

    for copy in sent:
        copy.wait_send()
    for i, r in enumerate(z_peers):
        fp_copy(i, my_r, r).wait_send()


def replicated(nr, nm, ensemble, obs_value, obs_error, obs_region, obs_cell, order, footprint):
    md, cd = ensemble.shape
    members, cells = md * nm, cd * nr
    total = order.shape[0]
    lines = [v.reshape(total // LANES, LANES) for v in (order, obs_region, obs_cell, obs_error, obs_value)]
    line = (total // LANES, LANES)
    chips = nm // CORES
    sends = (nr - 1) + nr * (chips - 1) + nr * chips
    return pl.pallas_call(
        functools.partial(kernel, nr, nm),
        out_shape=jax.ShapeDtypeStruct((md, cd), F32),
        in_specs=[pl.BlockSpec(memory_space=pltpu.HBM)] * 7,
        out_specs=pl.BlockSpec(memory_space=pltpu.VMEM),
        scratch_shapes=[
            pltpu.SMEM(footprint.shape, jnp.int32),
            pltpu.VMEM(line, jnp.int32),
            pltpu.VMEM(line, jnp.int32),
            pltpu.VMEM(line, jnp.int32),
            pltpu.VMEM(line, F32),
            pltpu.VMEM(line, F32),
            pltpu.SemaphoreType.DMA((7,)),
            pltpu.VMEM((nr, members, cd), F32),
            pltpu.VMEM((nr, 8, LANES), jnp.int32),
            pltpu.VMEM((8, LANES), jnp.int32),
            pltpu.VMEM((cells + cd, LANES), F32),
            pltpu.VMEM((cells + cd, cells), BF16),
            pltpu.VMEM((cells, members), F32),
            pltpu.VMEM((cells, members), F32),
            pltpu.VMEM((cells, 2 * members), BF16),
            pltpu.VMEM((cells, members), BF16),
            pltpu.VMEM((cells, members), BF16),
            pltpu.VMEM((cells, members), BF16),
            pltpu.VMEM((cells, members), BF16),
            pltpu.VMEM((members, cd), F32),
            pltpu.SemaphoreType.DMA((sends,)),
            pltpu.SemaphoreType.DMA((nr, nm)),
            pltpu.SemaphoreType.DMA((nr,)),
            pltpu.SemaphoreType.DMA((nr,)),
        ],
        compiler_params=pltpu.CompilerParams(
            collective_id=0, has_side_effects=True, vmem_limit_bytes=48 * 1024 * 1024
        ),
    )(*[pltpu.with_memory_space_constraint(v, pltpu.HBM) for v in (footprint, ensemble, *lines)])


def sharded(ensemble, obs_value, obs_error, obs_region, obs_cell, order, footprint):
    mem_dev, cell_count = ensemble.shape
    members = mem_dev * lax.axis_size("member")
    tile_count = cell_count // STILE
    state = ensemble
    region = lax.axis_index("region")
    offsets = jnp.arange(OTILE, dtype=jnp.int32)
    for batch_no in range(BATCHES):
        chosen = order[batch_no * NOBS : (batch_no + 1) * NOBS]
        owned_here = obs_region[chosen] == region
        picked = jnp.where(owned_here[None, :], jnp.take(state, obs_cell[chosen], axis=1), 0.0)
        priors = lax.psum(picked, "region")
        obs_index = (footprint[batch_no][:, :, None] * OTILE + offsets[None, None, :]).reshape(
            tile_count, FOOT * OTILE
        )
        state_tiles = state.reshape(mem_dev, tile_count, STILE)
        s_one = jnp.sum(priors, axis=0)
        s_two = jnp.sum(priors * priors, axis=0)
        s_one, s_two = lax.psum((s_one, s_two), "member")
        obs_mean = s_one / members
        obs_pert = priors - obs_mean[None, :]
        obs_tiles = jnp.take(obs_pert, obs_index, axis=1)
        partial_value = jnp.einsum(
            "mtj,mtc->tjc", obs_tiles, state_tiles, precision=lax.Precision.HIGHEST
        )
        summed = lax.psum(partial_value, "member")
        covariance = summed / (members - 1)
        obs_var = (s_two - s_one * obs_mean) / (members - 1)
        err_var = obs_error[chosen]
        obs_gain = 1.0 / (obs_var + err_var)
        shrink = 1.0 / (1.0 + jnp.sqrt(err_var * obs_gain))
        innovation = obs_value[chosen] - obs_mean
        weight = covariance * obs_gain[obs_index][:, :, None]
        mean_step = jnp.einsum(
            "tjc,tj->tc", weight, innovation[obs_index], precision=lax.Precision.HIGHEST
        )
        scaled = obs_tiles * shrink[obs_index][None, :, :]
        pert_step = jnp.einsum("mtj,tjc->mtc", scaled, weight, precision=lax.Precision.HIGHEST)
        state = (
            state + mean_step.reshape(cell_count)[None, :] - pert_step.reshape(mem_dev, cell_count)
        )
    return state


def solution(mesh):
    nr, nm = mesh.shape["region"], mesh.shape["member"]

    def per_device(ensemble, *rest):
        if 4 * ensemble.size * nr * nm <= REPLICATED_LIMIT:
            return replicated(nr, nm, ensemble, *rest)
        return sharded(ensemble, *rest)

    in_specs = (P("member", "region"), P(), P(), P(), P(), P(), P(None, "region", None))
    out_specs = P("member", "region")
    return jax.shard_map(
        per_device, mesh=mesh, in_specs=in_specs, out_specs=out_specs, check_vma=False
    )
```
